512 devices in a mesh: grow: 32 (over x_hi, y, core), gcol: 16 (over z, x_lo).
Axes of the slice: x: 4 (x_hi: 2, x_lo: 2; x = x_hi * 2 + x_lo), y: 8, z: 8, core: 2. Of those that a mesh axis runs over, the one named last changes fastest.
Arguments:
- coefficients: bfloat16 [20480, 49152], P('grow', 'gcol'), may hold values from -0.02734375 to 0.02734375
- tile_mask: int32 [160, 384], P('grow', 'gcol'), may hold values 0 or 1
- duals: float32 [20480], P('grow'), may hold values from -6 to 6
- costs: float32 [49152], P('gcol'), may hold values from -6 to 6
- primal: float32 [49152], P('gcol'), may hold values from 0.1 to 10
- fixed: int32 [49152], P('gcol'), may hold values 0 or 1
Outputs:
- normal_window: float32 [1024, 20480], P('gcol', 'grow')
- factor_window: float32 [1024, 20480], P('gcol', 'grow')
The draws below stay inside these ranges and needn't reach their ends.
All inputs are finite; a program needn't handle non-finite values. No bound on the sum of `tile_mask` or of `fixed` on one device may be relied on, other than what follows from the above.
Results may differ from the reference program's by a relative error of at most 0.0023.
Values may be sent and summed in bfloat16 or wider, within the bound.
A program may use at most 64 MiB of HBM per device.

```python
import math
import jax
import jax.numpy as jnp
from jax import lax

ORDER = 20480
PANEL = 512
TILE = 128
NCOL_DEV = 3072
NCOL = 49152
N_GROW = 32
N_GCOL = 16


def plant(drawn, own_key, least, largest):
    extent = drawn.shape
    place = [jax.random.randint(jax.random.fold_in(own_key, axis), (), 0, extent[axis]) for axis in range(len(extent))]
    drawn = drawn.at[tuple(place)].set(least)
    longest = extent.index(max(extent))
    place[longest] = (place[longest] + 1) % extent[longest]
    return drawn.at[tuple(place)].set(largest)


def steps_of(rng, extent, cuts, low, largest):
    loudness = 1.0
    for position, blocks in cuts:
        draws = jax.random.uniform(jax.random.fold_in(jax.random.fold_in(rng, 6), position), (blocks,), jnp.float32, low / len(cuts), largest / len(cuts))
        loudness = loudness * jnp.repeat(jnp.exp(draws), extent[position] // blocks).reshape((-1,) + (1,) * (len(extent) - 1 - position))
    return loudness


def bell_draw(key, shape, deviation, reach, pieces=(), kind=jnp.bfloat16):
    array = deviation * jax.random.normal(key, shape, jnp.float32)
    if pieces:
        array = array * steps_of(key, shape, pieces, -0.22, 0.18)
    return jnp.clip(array, -reach, reach).astype(kind)


def setup_inputs(seed: int = 0) -> dict:
    keys = jax.random.split(jax.random.key(seed), 7)
    coefficients = bell_draw(keys[0], (ORDER, NCOL), NCOL ** -0.5, 0.02734375, ((0, 32), (1, 16)))
    tile_mask = plant((jax.random.randint(keys[1], (ORDER // TILE, NCOL // TILE), 0, 4) < 3).astype(jnp.int32), jax.random.fold_in(keys[1], 1), 0, 1)
    duals = bell_draw(keys[2], (ORDER,), 1.0, 6.0, ((0, 32),), jnp.float32)
    costs = bell_draw(keys[3], (NCOL,), 1.0, 6.0, ((0, 16),), jnp.float32)
    primal = jnp.clip(jnp.exp(math.log(10.0) - 4.6051702 * jax.random.uniform(keys[4], (NCOL,), jnp.float32) ** steps_of(keys[4], (NCOL,), ((0, 16),), -0.2, 0.2)), 0.1, 10.0)
    fixed = plant((jax.random.randint(keys[5], (NCOL,), 0, 8) < 1).astype(jnp.int32), jax.random.fold_in(keys[5], 1), 0, 1)
    return dict(coefficients=coefficients, tile_mask=tile_mask, duals=duals, costs=costs, primal=primal, fixed=fixed)


SOFTNESS = 0.25
DIAGONAL_SHIFT = 0.5

def reference(coefficients, tile_mask, duals, costs, primal, fixed):
    rows_per = ORDER // N_GROW
    panel_per = PANEL // N_GROW
    tiles_per = NCOL_DEV // TILE

    def group(index, normal):
        start = (index * NCOL_DEV).astype(jnp.int32)
        block = lax.dynamic_slice_in_dim(coefficients, start, NCOL_DEV, 1)
        tiles = lax.dynamic_slice_in_dim(tile_mask, (index * tiles_per).astype(jnp.int32), tiles_per, 1)
        expanded = jnp.repeat(jnp.repeat(tiles, TILE, axis=0), TILE, axis=1)
        masked = block * expanded.astype(jnp.bfloat16)
        products = jnp.dot(duals, masked.astype(jnp.float32), precision=lax.Precision.HIGHEST)
        reduced = lax.dynamic_slice_in_dim(costs, start, NCOL_DEV) - products
        kept = (1 - lax.dynamic_slice_in_dim(fixed, start, NCOL_DEV)).astype(jnp.float32)
        scaling = kept * lax.dynamic_slice_in_dim(primal, start, NCOL_DEV) / jnp.sqrt(reduced * reduced + SOFTNESS)
        scaled = (masked.astype(jnp.float32) * scaling[None, :]).astype(jnp.bfloat16)
        window = masked.reshape(N_GROW, rows_per, NCOL_DEV)[:, :2 * panel_per].reshape(2 * PANEL, NCOL_DEV)
        return normal + lax.dot_general(window.astype(jnp.float32), scaled.astype(jnp.float32), (((1,), (1,)), ((), ())), preferred_element_type=jnp.float32)
    normal = lax.fori_loop(0, N_GCOL, group, jnp.zeros((2 * PANEL, ORDER), jnp.float32))
    split = normal.reshape(N_GROW, 2, panel_per, ORDER)
    panel = split[:, 0].reshape(PANEL, ORDER)
    trailing = split[:, 1].reshape(PANEL, ORDER)
    corner = panel.reshape(PANEL, N_GROW, rows_per)[:, :, :panel_per].reshape(PANEL, PANEL)
    shifted = 0.5 * (corner + corner.T) + DIAGONAL_SHIFT * jnp.eye(PANEL, dtype=jnp.float32)
    lower = jnp.linalg.cholesky(shifted)
    factor_panel = jax.scipy.linalg.solve_triangular(lower, panel, lower=True)
    edge = factor_panel.reshape(PANEL, N_GROW, rows_per)[:, :, panel_per:2 * panel_per].reshape(PANEL, PANEL)
    updated = trailing - jnp.dot(edge.T, factor_panel, precision=lax.Precision.HIGHEST)
    factor = jnp.stack([factor_panel.reshape(N_GROW, panel_per, ORDER), updated.reshape(N_GROW, panel_per, ORDER)], axis=1)
    return (normal, factor.reshape(2 * PANEL, ORDER))
```

```python
import functools

import jax
import jax.numpy as jnp
from jax import lax
from jax.experimental import pallas as pl
from jax.experimental.pallas import tpu as pltpu
from jax.sharding import PartitionSpec as P

PANEL = 512
SOFTNESS = 0.25
DIAGONAL_SHIFT = 0.5
CORES = 2
PLANES = 2
BLOCK = 128
MESH = pl.DeviceIdType.MESH
HIGHEST = lax.Precision.HIGHEST
NT = (((1,), (1,)), ((), ()))


def copy_to(src, dst, send_sem, recv_sem, g, c):
    return pltpu.make_async_remote_copy(
        src_ref=src, dst_ref=dst, send_sem=send_sem, recv_sem=recv_sem, device_id=(g, c), device_id_type=MESH
    )


class Place:
    def __init__(self, row_count, col_count):
        self.y_count = row_count // (CORES * PLANES)
        self.row_count, self.col_count = row_count, col_count
        self.g = lax.axis_index("grow")
        self.c = lax.axis_index("gcol")
        self.core = lax.rem(self.g, CORES)
        chip = self.g // CORES
        self.y = lax.rem(chip, self.y_count)
        self.plane = chip // self.y_count

    def at(self, plane, y, core):
        return (plane * self.y_count + y) * CORES + core

    def ring(self, hop):
        return lax.rem(self.y + hop + 2 * self.y_count, self.y_count)


def enter(me, wait):
    barrier = pltpu.get_barrier_semaphore()
    if not wait:
        for k in range(1, me.row_count):
            pl.semaphore_signal(
                barrier, inc=1, device_id=(lax.rem(me.g + k, me.row_count), me.c), device_id_type=MESH
            )
        for k in range(1, me.col_count):
            pl.semaphore_signal(
                barrier, inc=1, device_id=(me.g, lax.rem(me.c + k, me.col_count)), device_id_type=MESH
            )
    else:
        pl.semaphore_wait(barrier, me.row_count + me.col_count - 2)


def window_kernel(
    row_count, col_count, panel_per,
    coef, mask, duals, costs, primal, fixed,
    normal,
    a, win, dcol, pa, pb, scale, part, own, out, inc,
    load_sem, win_send, win_recv, pa_send, pa_recv, pb_send, pb_recv, rs_send, rs_recv,
):
    me = Place(row_count, col_count)
    rows, columns = a.shape
    window = 2 * panel_per
    tile_rows, tile_cols = mask.shape
    side = rows // tile_rows
    yc = me.y_count

    enter(me, False)
    first = pltpu.make_async_copy(coef.at[pl.ds(0, window)], a.at[pl.ds(0, window)], load_sem.at[0])
    rest = pltpu.make_async_copy(
        coef.at[pl.ds(window, rows - window)], a.at[pl.ds(window, rows - window)], load_sem.at[1]
    )
    first.start()
    rest.start()
    first.wait()

    def mask_window(k, _):
        sl = pl.ds(pl.multiple_of(k * side, side), side)
        m = mask[0, k].astype(jnp.float32)
        win[me.g, :, sl] = (a[0:window, sl].astype(jnp.float32) * m).astype(jnp.bfloat16)
        return 0

    lax.fori_loop(0, tile_cols, mask_window, 0)
    enter(me, True)

    sends = []

    def send_window(slot, g, c):
        cp = copy_to(win.at[slot], win.at[slot], win_send.at[len(sends)], win_recv.at[slot], g, c)
        cp.start()
        sends.append(cp)

    def got_window(slot):
        copy_to(win.at[slot], win.at[slot], win_send.at[0], win_recv.at[slot], me.g, me.c).wait_recv()

    sibling = me.at(me.plane, me.y, 1 - me.core)
    right = me.at(me.plane, me.ring(1), me.core)
    left = me.at(me.plane, me.ring(-1), me.core)
    other = 1 - me.plane
    reach = {0: (yc // 2, (yc - 1) // 2), 1: ((yc - 1) // 2, yc // 2)}

    def pass_on(kind, hop_right, hop_left, which):
        plane = me.plane if kind == 0 else other
        if which in (0, 1) and hop_right < reach[kind][0]:
            send_window(me.at(plane, me.ring(-hop_right), me.core), right, me.c)
        if which in (0, 2) and hop_left < reach[kind][1]:
            send_window(me.at(plane, me.ring(hop_left), me.core), left, me.c)

    send_window(me.g, me.at(other, me.y, me.core), me.c)
    pass_on(0, 0, 0, 0)
    send_window(me.g, sibling, me.c)

    for i in range(tile_rows):
        dcol[i * side:(i + 1) * side, :] = jnp.transpose(jnp.broadcast_to(duals[i:i + 1, :], (side, side)))
    rest.wait()
    q = me.plane * CORES + me.core

    def products(k, _):
        sl = pl.ds(pl.multiple_of(k * side, side), side)
        total = jnp.zeros((8, side), jnp.float32)
        for i in range(tile_rows):
            block = slice(i * side, (i + 1) * side)
            x = a[block, sl].astype(jnp.float32) * mask[i, k].astype(jnp.float32)
            a[block, sl] = x.astype(jnp.bfloat16)
            total += (x * dcol[block, :]).reshape(side // 8, 8, side).sum(axis=0)
        pa[q, :, sl] = total.sum(axis=0, keepdims=True)
        return 0

    lax.fori_loop(0, tile_cols, products, 0)

    small = []
    n = 0
    for dp in range(PLANES):
        for dc in range(CORES):
            if dp == 0 and dc == 0:
                continue
            plane = lax.rem(me.plane + dp, PLANES)
            core = lax.rem(me.core + dc, CORES)
            cp = copy_to(pa.at[q], pa.at[q], pa_send.at[n], pa_recv.at[q], me.at(plane, me.y, core), me.c)
            cp.start()
            small.append(cp)
            n += 1

    partner = me.at(other, me.y, me.core)
    got_window(partner)
    pass_on(1, 0, 0, 0)
    send_window(partner, sibling, me.c)

    for dp in range(PLANES):
        for dc in range(CORES):
            if dp == 0 and dc == 0:
                continue
            s = lax.rem(me.plane + dp, PLANES) * CORES + lax.rem(me.core + dc, CORES)
            copy_to(pa.at[s], pa.at[s], pa_send.at[0], pa_recv.at[s], me.g, me.c).wait_recv()
    total = pa[0]
    for s in range(1, PLANES * CORES):
        total = total + pa[s]
    pb[me.y] = total
    for k in range(1, yc):
        cp = copy_to(
            pb.at[me.y], pb.at[me.y], pb_send.at[k], pb_recv.at[me.y], me.at(me.plane, me.ring(k), me.core), me.c
        )
        cp.start()
        small.append(cp)

    def service(hop):
        for kind in (0, 1):
            plane = me.plane if kind == 0 else other
            if hop <= reach[kind][0]:
                slot = me.at(plane, me.ring(-hop), me.core)
                got_window(slot)
                pass_on(kind, hop, 0, 1)
                send_window(slot, sibling, me.c)
            if hop <= reach[kind][1]:
                slot = me.at(plane, me.ring(hop), me.core)
                got_window(slot)
                pass_on(kind, 0, hop, 2)
                send_window(slot, sibling, me.c)

    service(1)
    for k in range(1, yc):
        s = me.ring(k)
        copy_to(pb.at[s], pb.at[s], pb_send.at[0], pb_recv.at[s], me.g, me.c).wait_recv()
    total = pb[0]
    for s in range(1, yc):
        total = total + pb[s]
    reduced = costs[...] - total
    scale[...] = (1 - fixed[...]).astype(jnp.float32) * primal[...] / jnp.sqrt(reduced * reduced + SOFTNESS)

    def rescale(k, _):
        sl = pl.ds(pl.multiple_of(k * side, side), side)
        s = jnp.broadcast_to(scale[:, sl], (side, side))
        for i in range(tile_rows):
            block = slice(i * side, (i + 1) * side)
            a[block, sl] = (a[block, sl].astype(jnp.float32) * s).astype(jnp.bfloat16)
        return 0

    lax.fori_loop(0, tile_cols, rescale, 0)
    for hop in range(2, yc // 2 + 1):
        service(hop)
    for plane in range(PLANES):
        for y in range(yc):
            got_window(me.at(plane, y, 1 - me.core))

    owners = min(4, col_count)
    groups = col_count // owners
    blocks = row_count // col_count
    mine = blocks * window
    depth = min(512, columns)
    inc[me.c] = jnp.zeros(inc.shape[1:], inc.dtype)

    def multiply(step, _):
        group = lax.rem(me.c // owners + step, groups)
        part[...] = jnp.zeros_like(part)

        def deep(k, _):
            sl = pl.ds(pl.multiple_of(k * depth, depth), depth)
            lhs = win[pl.ds(group * (owners * blocks), owners * blocks), :, sl].reshape(owners * mine, depth)
            part[...] += lax.dot_general(lhs, a[:, sl], NT, preferred_element_type=jnp.float32)
            return 0

        lax.fori_loop(0, columns // depth, deep, 0)
        for k in range(owners):
            owner = group * owners + k
            piece = part[k * mine:(k + 1) * mine, :]
            out[owner] = piece.astype(jnp.bfloat16)

            @pl.when(owner == me.c)
            def _():
                own[...] = piece

            @pl.when(owner != me.c)
            def _():
                copy_to(out.at[owner], inc.at[me.c], rs_send.at[owner], rs_recv.at[me.c], me.g, owner).start()

        return 0

    lax.fori_loop(0, groups, multiply, 0)
    for s in range(col_count):
        @pl.when(me.c != s)
        def _():
            copy_to(out.at[s], inc.at[s], rs_send.at[s], rs_recv.at[s], me.g, me.c).wait_recv()

    total = own[...]
    for s in range(col_count):
        total = total + inc[s].astype(jnp.float32)
    normal[...] = total

    for s in range(col_count):
        @pl.when(me.c != s)
        def _():
            copy_to(out.at[s], inc.at[s], rs_send.at[s], rs_recv.at[s], me.g, me.c).wait_send()
    for cp in small + sends:
        cp.wait_send()


def gather_kernel(
    row_count, col_count, panel_per,
    normal,
    panel, corner, edge,
    epiece, panel_send, panel_recv, corner_send, corner_recv, edge_send, edge_recv,
):
    me = Place(row_count, col_count)
    blocks = row_count // col_count
    enter(me, False)
    for b in range(blocks):
        panel[me.c, b * panel_per:(b + 1) * panel_per, :] = normal[2 * b * panel_per:(2 * b + 1) * panel_per, :]
    enter(me, True)
    sends = []
    for k in range(1, col_count):
        cp = copy_to(
            panel.at[me.c], panel.at[me.c], panel_send.at[k], panel_recv.at[me.c],
            me.g, lax.rem(me.c + k, col_count),
        )
        cp.start()
        sends.append(cp)
    for k in range(1, col_count):
        s = lax.rem(me.c + k, col_count)
        copy_to(panel.at[s], panel.at[s], panel_send.at[0], panel_recv.at[s], me.g, me.c).wait_recv()
    head = panel[:, :, 0:BLOCK].reshape(panel.shape[0] * panel.shape[1], BLOCK)
    turned = jnp.transpose(head)
    corner[me.g] = turned[0:panel_per]
    epiece[...] = turned[panel_per:2 * panel_per]
    sibling = me.at(me.plane, me.y, 1 - me.core)

    def send_corner(slot, g):
        cp = copy_to(corner.at[slot], corner.at[slot], corner_send.at[len(sends) - col_count + 1], corner_recv.at[slot], g, me.c)
        cp.start()
        sends.append(cp)

    peers = [
        me.at(lax.rem(me.plane + p, PLANES), me.ring(k), me.core)
        for k in range(me.y_count) for p in range(PLANES) if k or p
    ]
    for peer in peers:
        send_corner(me.g, peer)
    send_corner(me.g, sibling)

    source = me.g // CORES == me.c

    def edge_copy(n, g):
        return copy_to(edge.at[me.core], edge.at[me.core], edge_send.at[n], edge_recv.at[me.core], g, me.c)

    @pl.when(source)
    def _():
        edge[me.core] = epiece[...]
        for n, peer in enumerate(peers):
            edge_copy(n, peer).start()

    @pl.when(jnp.logical_not(source))
    def _():
        edge_copy(0, me.g).wait_recv()

    edge_copy(len(peers), sibling).start()

    for peer in peers:
        copy_to(corner.at[peer], corner.at[peer], corner_send.at[0], corner_recv.at[peer], me.g, me.c).wait_recv()
        send_corner(peer, sibling)
    for plane in range(PLANES):
        for y in range(me.y_count):
            s = me.at(plane, y, 1 - me.core)
            copy_to(corner.at[s], corner.at[s], corner_send.at[0], corner_recv.at[s], me.g, me.c).wait_recv()
    other = 1 - me.core
    copy_to(edge.at[other], edge.at[other], edge_send.at[0], edge_recv.at[other], me.g, me.c).wait_recv()

    @pl.when(source)
    def _():
        for n, peer in enumerate(peers):
            edge_copy(n, peer).wait_send()

    edge_copy(len(peers), sibling).wait_send()
    for cp in sends:
        cp.wait_send()


def invert_block(d):
    n = d.shape[0]
    lane = lax.broadcasted_iota(jnp.int32, (8, n), 1)
    sub = lax.broadcasted_iota(jnp.int32, (8, n), 0)
    rows = [d[8 * i:8 * i + 8, :] for i in range(n // 8)]
    pivots = []
    for b in range(n // 8):
        pivot = jnp.ones((8, n), jnp.float32)
        for s in range(8):
            j = 8 * b + s
            row = rows[b][s:s + 1, :]
            p = jnp.broadcast_to(rows[b][s:s + 1, j:j + 1], (1, n))
            row = jnp.where(lane[0:1] == j, 1.0, row) / p
            row = jnp.broadcast_to(row, (8, n))
            pivot = jnp.where(sub == s, jnp.broadcast_to(p, (8, n)), pivot)
            for i in range(b, n // 8):
                col = jnp.broadcast_to(rows[i][:, j:j + 1], (8, n))
                gone = lane == j
                if i == b:
                    col = jnp.where(sub > s, col, 0.0)
                    gone = gone & (sub > s)
                rows[i] = jnp.where(gone, 0.0, rows[i]) - col * row
        pivots.append(pivot)
    done = []
    for b in range(n // 8):
        r = sub + 8 * b
        low = jnp.where(lane < r, rows[b], jnp.where(lane == r, 1.0, 0.0))
        done.append(low / jnp.sqrt(pivots[b]))
    return jnp.concatenate(done, axis=0)


def dot32(x, y, dims=(((1,), (0,)), ((), ()))):
    return lax.dot_general(x, y, dims, precision=HIGHEST, preferred_element_type=jnp.float32)


def factor_kernel(col_count, panel_per, normal, panel, corner, edge, factor, s):
    n = s.shape[0]
    c = lax.axis_index("gcol")
    own = n // col_count
    row_id = lax.broadcasted_iota(jnp.int32, (n, n), 0)
    col_id = lax.broadcasted_iota(jnp.int32, (n, n), 1)
    given = corner[...]
    s[...] = 0.5 * (given + jnp.transpose(given)) + jnp.where(row_id == col_id, DIAGONAL_SHIFT, 0.0)

    def step(k, _):
        at = pl.ds(pl.multiple_of(k * BLOCK, BLOCK), BLOCK)
        inverse = invert_block(s[at, at])
        below = lax.broadcasted_iota(jnp.int32, (n, BLOCK), 0) >= (k + 1) * BLOCK
        column = jnp.where(below, dot32(s[:, at], inverse, NT), 0.0)
        s[at, at] = jnp.where(
            lax.broadcasted_iota(jnp.int32, (BLOCK, BLOCK), 0) == lax.broadcasted_iota(jnp.int32, (BLOCK, BLOCK), 1),
            1.0, 0.0,
        )
        row = dot32(inverse, s[at, :])
        s[at, :] = row
        s[:, at] = jnp.where(below, 0.0, s[:, at])
        s[...] = s[...] - dot32(column, row)
        return 0

    lax.fori_loop(0, n // BLOCK, step, 0)
    s[...] = jnp.where(col_id <= row_id, s[...], 0.0)
    inverse = s[...]
    turned_edge = dot32(edge[...], inverse, NT)
    weights = jnp.concatenate(
        [s[pl.ds(pl.multiple_of(c * own, own), own), :], dot32(turned_edge, inverse)], axis=0
    )
    made = dot32(weights, panel[...])
    for b in range(own // panel_per):
        at = b * panel_per
        factor[2 * at:2 * at + panel_per, :] = made[at:at + panel_per]
        factor[2 * at + panel_per:2 * at + 2 * panel_per, :] = (
            normal[2 * at + panel_per:2 * at + 2 * panel_per, :] - made[own + at:own + at + panel_per]
        )


def shards(row_count, col_count, coefficients, tile_mask, duals, costs, primal, fixed):
    rows, columns = coefficients.shape
    panel_per = PANEL // row_count
    window = 2 * panel_per
    blocks = row_count // col_count
    mine = blocks * window
    y_count = row_count // (CORES * PLANES)
    vmem, smem, anywhere = (pl.BlockSpec(memory_space=m) for m in (pltpu.VMEM, pltpu.SMEM, pl.ANY))
    dma = pltpu.SemaphoreType.DMA
    f32, bf16 = jnp.float32, jnp.bfloat16
    normal = pl.pallas_call(
        functools.partial(window_kernel, row_count, col_count, panel_per),
        out_shape=jax.ShapeDtypeStruct((mine, rows), f32),
        in_specs=[anywhere, smem, vmem, vmem, vmem, vmem],
        out_specs=vmem,
        scratch_shapes=[
            pltpu.VMEM((rows, columns), bf16),
            pltpu.VMEM((row_count, window, columns), bf16),
            pltpu.VMEM((rows, BLOCK), f32),
            pltpu.VMEM((PLANES * CORES, 1, columns), f32),
            pltpu.VMEM((y_count, 1, columns), f32),
            pltpu.VMEM((1, columns), f32),
            pltpu.VMEM((min(4, col_count) * mine, rows), f32),
            pltpu.VMEM((mine, rows), f32),
            pltpu.VMEM((col_count, mine, rows), bf16),
            pltpu.VMEM((col_count, mine, rows), bf16),
            dma((2,)),
            dma((2 * row_count,)), dma((row_count,)),
            dma((PLANES * CORES,)), dma((PLANES * CORES,)),
            dma((y_count,)), dma((y_count,)),
            dma((col_count,)), dma((col_count,)),
        ],
        compiler_params=pltpu.CompilerParams(collective_id=0, has_side_effects=True, vmem_limit_bytes=40 << 20),
        name="window",
    )(
        coefficients, tile_mask, duals.reshape(rows // BLOCK, BLOCK), costs.reshape(1, columns),
        primal.reshape(1, columns), fixed.reshape(1, columns),
    )
    own = PANEL // col_count
    panel, corner, edge = pl.pallas_call(
        functools.partial(gather_kernel, row_count, col_count, panel_per),
        out_shape=(
            jax.ShapeDtypeStruct((col_count, own, rows), f32),
            jax.ShapeDtypeStruct((row_count, panel_per, PANEL), f32),
            jax.ShapeDtypeStruct((blocks, panel_per, PANEL), f32),
        ),
        in_specs=[vmem],
        out_specs=(vmem, vmem, vmem),
        scratch_shapes=[
            pltpu.VMEM((panel_per, PANEL), f32),
            dma((col_count,)), dma((col_count,)),
            dma((row_count + 1,)), dma((row_count,)),
            dma((row_count // 2,)), dma((CORES,)),
        ],
        compiler_params=pltpu.CompilerParams(collective_id=1, has_side_effects=True, vmem_limit_bytes=24 << 20),
        name="gather",
    )(normal)
    factor = pl.pallas_call(
        functools.partial(factor_kernel, col_count, panel_per),
        out_shape=jax.ShapeDtypeStruct((mine, rows), f32),
        in_specs=[vmem] * 4,
        out_specs=vmem,
        scratch_shapes=[pltpu.VMEM((PANEL, PANEL), f32)],
        compiler_params=pltpu.CompilerParams(vmem_limit_bytes=32 << 20),
        name="factor",
    )(normal, panel.reshape(PANEL, rows), corner.reshape(PANEL, PANEL), edge.reshape(own, PANEL))
    return normal, factor


def solution(mesh):
    placed = (P("grow", "gcol"), P("grow", "gcol"), P("grow"), P("gcol"), P("gcol"), P("gcol"))
    return jax.shard_map(
        functools.partial(shards, mesh.shape["grow"], mesh.shape["gcol"]),
        mesh=mesh,
        in_specs=placed,
        out_specs=(P("gcol", "grow"), P("gcol", "grow")),
        check_vma=False,
    )
```

```python
import functools

import jax
import jax.numpy as jnp
from jax import lax
from jax.experimental import pallas as pl
from jax.experimental.pallas import tpu as pltpu
from jax.sharding import PartitionSpec as P

PANEL = 512
SOFTNESS = 0.25
DIAGONAL_SHIFT = 0.5
CORES = 2
PLANES = 2
BLOCK = 128
MESH = pl.DeviceIdType.MESH
HIGHEST = lax.Precision.HIGHEST
NT = (((1,), (1,)), ((), ()))
NN = (((1,), (0,)), ((), ()))


def copy_to(src, dst, send_sem, recv_sem, g, c):
    return pltpu.make_async_remote_copy(
        src_ref=src, dst_ref=dst, send_sem=send_sem, recv_sem=recv_sem, device_id=(g, c), device_id_type=MESH
    )


class Place:
    def __init__(self, row_count, col_count):
        self.y_count = row_count // (CORES * PLANES)
        self.row_count, self.col_count = row_count, col_count
        self.g = lax.axis_index("grow")
        self.c = lax.axis_index("gcol")
        self.core = lax.rem(self.g, CORES)
        self.chip = self.g // CORES
        self.y = lax.rem(self.chip, self.y_count)
        self.plane = self.chip // self.y_count
        self.other = 1 - self.plane
        self.sibling = self.at(self.plane, self.y, 1 - self.core)
        self.partner = self.at(self.other, self.y, self.core)

    def at(self, plane, y, core):
        return (plane * self.y_count + y) * CORES + core

    def ring(self, hop):
        return lax.rem(self.y + hop + 2 * self.y_count, self.y_count)


def greet(me):
    barrier = pltpu.get_barrier_semaphore()
    for k in range(1, me.row_count):
        pl.semaphore_signal(barrier, inc=1, device_id=(lax.rem(me.g + k, me.row_count), me.c), device_id_type=MESH)
    for k in range(1, me.col_count):
        pl.semaphore_signal(barrier, inc=1, device_id=(me.g, lax.rem(me.c + k, me.col_count)), device_id_type=MESH)


def greeted(me):
    pl.semaphore_wait(pltpu.get_barrier_semaphore(), me.row_count + me.col_count - 2)


def window_kernel(
    row_count, col_count, panel_per,
    coef, mask_in, duals_in, costs_in, primal_in, fixed_in,
    normal, corner, epiece,
    a, win, mask, duals, costs, primal, fixed, dcol, pa, pb, scale, part, own, out, inc, qacc, qout, qin,
    load_sem, win_send, win_recv, pa_send, pa_recv, pb_send, pb_recv, rs_send, rs_recv, q_send, q_recv,
    t_send, t_recv, e_send, e_recv, cor_send, cor_recv,
):
    me = Place(row_count, col_count)
    rows, columns = a.shape
    window = 2 * panel_per
    tile_rows, tile_cols = mask.shape
    side = rows // tile_rows
    yc = me.y_count

    loads = [
        pltpu.make_async_copy(src, dst, load_sem.at[n])
        for n, (src, dst) in enumerate([
            (mask_in, mask),
            (coef.at[pl.ds(0, window)], a.at[pl.ds(0, window)]),
            (duals_in, duals),
            (coef.at[pl.ds(window, rows - window)], a.at[pl.ds(window, rows - window)]),
            (costs_in, costs), (primal_in, primal), (fixed_in, fixed),
        ])
    ]
    for load in loads:
        load.start()
    greet(me)
    loads[0].wait()
    loads[1].wait()

    def mask_window(k, _):
        sl = pl.ds(pl.multiple_of(k * side, side), side)
        m = mask[0, k].astype(jnp.float32)
        win[me.g, :, sl] = (a[0:window, sl].astype(jnp.float32) * m).astype(jnp.bfloat16)
        return 0

    lax.fori_loop(0, tile_cols, mask_window, 0)
    greeted(me)

    sends = []

    def send_window(slot, g):
        cp = copy_to(win.at[slot], win.at[slot], win_send.at[len(sends)], win_recv.at[slot], g, me.c)
        cp.start()
        sends.append(cp)

    def got_window(slot):
        copy_to(win.at[slot], win.at[slot], win_send.at[0], win_recv.at[slot], me.g, me.c).wait_recv()

    right = me.at(me.plane, me.ring(1), me.core)
    left = me.at(me.plane, me.ring(-1), me.core)
    reach = ((yc // 2, (yc - 1) // 2), ((yc - 1) // 2, yc // 2))
    planes = (me.plane, me.other)

    def pass_right(kind, hop):
        if hop < reach[kind][0]:
            send_window(me.at(planes[kind], me.ring(-hop), me.core), right)

    def pass_left(kind, hop):
        if hop < reach[kind][1]:
            send_window(me.at(planes[kind], me.ring(hop), me.core), left)

    send_window(me.g, me.partner)
    pass_right(0, 0)
    pass_left(0, 0)
    send_window(me.g, me.sibling)

    loads[2].wait()
    for i in range(tile_rows):
        dcol[i * side:(i + 1) * side, :] = jnp.transpose(jnp.broadcast_to(duals[i:i + 1, :], (side, side)))
    loads[3].wait()
    q = me.plane * CORES + me.core

    def products(k, _):
        sl = pl.ds(pl.multiple_of(k * side, side), side)
        total = jnp.zeros((8, side), jnp.float32)
        for i in range(tile_rows):
            block = slice(i * side, (i + 1) * side)
            x = a[block, sl].astype(jnp.float32) * mask[i, k].astype(jnp.float32)
            a[block, sl] = x.astype(jnp.bfloat16)
            total += (x * dcol[block, :]).reshape(side // 8, 8, side).sum(axis=0)
        pa[q, :, sl] = total.sum(axis=0, keepdims=True)
        return 0

    lax.fori_loop(0, tile_cols, products, 0)

    quad = [
        (lax.rem(me.plane + dp, PLANES), lax.rem(me.core + dc, CORES))
        for dp in range(PLANES) for dc in range(CORES) if dp or dc
    ]
    for n, (plane, core) in enumerate(quad):
        cp = copy_to(pa.at[q], pa.at[q], pa_send.at[n], pa_recv.at[q], me.at(plane, me.y, core), me.c)
        cp.start()

    got_window(me.partner)
    pass_right(1, 0)
    pass_left(1, 0)
    send_window(me.partner, me.sibling)

    for plane, core in quad:
        s = plane * CORES + core
        copy_to(pa.at[s], pa.at[s], pa_send.at[0], pa_recv.at[s], me.g, me.c).wait_recv()
    total = pa[0]
    for s in range(1, PLANES * CORES):
        total = total + pa[s]
    pb[me.y] = total
    small = []
    for k in range(1, yc):
        cp = copy_to(
            pb.at[me.y], pb.at[me.y], pb_send.at[k], pb_recv.at[me.y], me.at(me.plane, me.ring(k), me.core), me.c
        )
        cp.start()
        small.append(cp)

    def service(hop):
        for kind in (0, 1):
            if hop <= reach[kind][0]:
                slot = me.at(planes[kind], me.ring(-hop), me.core)
                got_window(slot)
                pass_right(kind, hop)
                send_window(slot, me.sibling)
            if hop <= reach[kind][1]:
                slot = me.at(planes[kind], me.ring(hop), me.core)
                got_window(slot)
                pass_left(kind, hop)
                send_window(slot, me.sibling)

    def chips_at(hop):
        chips = []
        for kind in (0, 1):
            if hop <= reach[kind][0]:
                chips.append((planes[kind], me.ring(-hop)))
            if hop and hop <= reach[kind][1]:
                chips.append((planes[kind], me.ring(hop)))
        return chips

    service(1)
    for k in range(1, yc):
        s = me.ring(k)
        copy_to(pb.at[s], pb.at[s], pb_send.at[0], pb_recv.at[s], me.g, me.c).wait_recv()
    total = pb[0]
    for s in range(1, yc):
        total = total + pb[s]
    for load in loads[4:]:
        load.wait()
    reduced = costs[...] - total
    scale[...] = (1 - fixed[...]).astype(jnp.float32) * primal[...] / jnp.sqrt(reduced * reduced + SOFTNESS)

    def rescale(k, _):
        sl = pl.ds(pl.multiple_of(k * side, side), side)
        s = jnp.broadcast_to(scale[:, sl], (side, side))
        for i in range(tile_rows):
            block = slice(i * side, (i + 1) * side)
            a[block, sl] = (a[block, sl].astype(jnp.float32) * s).astype(jnp.bfloat16)
        return 0

    lax.fori_loop(0, tile_cols, rescale, 0)

    blocks = row_count // col_count
    mine = blocks * window
    depth = min(512, columns)
    inc[me.c] = jnp.zeros(inc.shape[1:], inc.dtype)

    def multiply(chips):
        for plane, y in chips:
            @pl.when((plane * yc + y) != me.chip)
            def _():
                got_window(me.at(plane, y, 1 - me.core))

            @pl.when((plane * yc + y) == me.chip)
            def _():
                got_window(me.sibling)
        owners = [plane * yc + y for plane, y in chips]
        tall = len(owners) * mine
        part[0:tall, :] = jnp.zeros((tall, rows), jnp.float32)

        def deep(k, _):
            sl = pl.ds(pl.multiple_of(k * depth, depth), depth)
            lhs = jnp.concatenate(
                [win[pl.ds(o * blocks, blocks), :, sl].reshape(mine, depth) for o in owners], axis=0
            )
            part[0:tall, :] += lax.dot_general(lhs, a[:, sl], NT, preferred_element_type=jnp.float32)
            return 0

        lax.fori_loop(0, columns // depth, deep, 0)
        for k, owner in enumerate(owners):
            piece = part[k * mine:(k + 1) * mine, :]
            out[owner] = piece.astype(jnp.bfloat16)

            @pl.when(owner == me.c)
            def _():
                own[...] = piece

            @pl.when(owner != me.c)
            def _():
                copy_to(out.at[owner], inc.at[me.c], rs_send.at[owner], rs_recv.at[me.c], me.g, owner).start()

    last = yc // 2
    if last == 1:
        multiply(chips_at(0))
    for hop in range(2, last + 1):
        if hop == last:
            multiply(chips_at(hop - 1))
            service(hop)
        else:
            service(hop)
            if hop == 2:
                multiply(chips_at(0))
            multiply(chips_at(hop - 1))
    if last == 2:
        multiply(chips_at(0))
    multiply(chips_at(last))

    qacc[...] = jnp.zeros_like(qacc)

    def head(k, _):
        sl = pl.ds(pl.multiple_of(k * depth, depth), depth)
        rhs = win[:, 0:panel_per, sl].reshape(row_count * panel_per, depth)
        qacc[...] += lax.dot_general(a[0:window, sl], rhs, NT, preferred_element_type=jnp.float32)
        return 0

    lax.fori_loop(0, columns // depth, head, 0)
    wide = qacc.shape[1] // BLOCK
    half = col_count // 2
    for t in range(col_count):
        i, j = t // wide, t % wide
        qout[t] = qacc[8 * i:8 * i + 8, BLOCK * j:BLOCK * j + BLOCK]
    qin[me.c] = qout[me.c]
    for k in range(1, col_count):
        t = lax.rem(me.c + k, col_count)
        copy_to(qout.at[t], qin.at[me.c], q_send.at[k], q_recv.at[me.c], me.g, t).start()
    for k in range(1, col_count):
        s = lax.rem(me.c + k, col_count)
        copy_to(qin.at[s], qin.at[s], q_send.at[0], q_recv.at[s], me.g, me.c).wait_recv()
    tile = qin[0]
    for s in range(1, col_count):
        tile = tile + qin[s]

    in_corner = me.c < half
    home = me.chip

    @pl.when(in_corner)
    def _():
        corner[me.g, me.c] = tile
        for k in range(1, col_count):
            copy_to(
                corner.at[me.g, me.c], corner.at[me.g, me.c], t_send.at[k], t_recv.at[me.c],
                me.g, lax.rem(me.c + k, col_count),
            ).start()

    @pl.when(jnp.logical_not(in_corner))
    def _():
        epiece[me.c - half] = tile

        @pl.when(me.c != home)
        def _():
            copy_to(
                epiece.at[me.c - half], epiece.at[me.c - half], e_send.at[0], e_recv.at[me.c - half], me.g, home
            ).start()

    for s in range(half):
        @pl.when(me.c != s)
        def _():
            copy_to(corner.at[me.g, s], corner.at[me.g, s], t_send.at[0], t_recv.at[s], me.g, me.c).wait_recv()

    cor = []

    def send_corner(slot, g):
        cp = copy_to(corner.at[slot], corner.at[slot], cor_send.at[len(cor)], cor_recv.at[slot], g, me.c)
        cp.start()
        cor.append(cp)

    def got_corner(slot):
        copy_to(corner.at[slot], corner.at[slot], cor_send.at[0], cor_recv.at[slot], me.g, me.c).wait_recv()

    for k in range(1, yc):
        send_corner(me.g, me.at(me.plane, me.ring(k), me.core))
    send_corner(me.g, me.partner)
    send_corner(me.g, me.sibling)
    for k in range(1, yc):
        slot = me.at(me.plane, me.ring(k), me.core)
        got_corner(slot)
        send_corner(slot, me.partner)
        send_corner(slot, me.sibling)
    for k in range(yc):
        slot = me.at(me.other, me.ring(k), me.core)
        got_corner(slot)
        send_corner(slot, me.sibling)

    for s in range(col_count):
        @pl.when(me.c != s)
        def _():
            copy_to(out.at[s], inc.at[s], rs_send.at[s], rs_recv.at[s], me.g, me.c).wait_recv()

    total = own[...]
    for s in range(col_count):
        total = total + inc[s].astype(jnp.float32)
    normal[...] = total

    for plane in range(PLANES):
        for y in range(yc):
            got_corner(me.at(plane, y, 1 - me.core))

    @pl.when(me.c == home)
    def _():
        for t in range(half):
            @pl.when(me.c != half + t)
            def _():
                copy_to(epiece.at[t], epiece.at[t], e_send.at[0], e_recv.at[t], me.g, me.c).wait_recv()

    @pl.when(jnp.logical_not(in_corner) & (me.c != home))
    def _():
        copy_to(epiece.at[0], epiece.at[0], e_send.at[0], e_recv.at[0], me.g, home).wait_send()

    @pl.when(in_corner)
    def _():
        for k in range(1, col_count):
            copy_to(qout.at[0], qout.at[0], t_send.at[k], t_recv.at[0], me.g, me.c).wait_send()

    for s in range(col_count):
        @pl.when(me.c != s)
        def _():
            copy_to(out.at[s], inc.at[s], rs_send.at[s], rs_recv.at[s], me.g, me.c).wait_send()
    for k in range(1, col_count):
        copy_to(qout.at[0], qout.at[0], q_send.at[k], q_recv.at[0], me.g, me.c).wait_send()
    for n in range(len(quad)):
        copy_to(pa.at[0], pa.at[0], pa_send.at[n], pa_recv.at[0], me.g, me.c).wait_send()
    for cp in small + sends + cor:
        cp.wait_send()


def invert_block(d):
    n = d.shape[0]
    lane = lax.broadcasted_iota(jnp.int32, (8, n), 1)
    sub = lax.broadcasted_iota(jnp.int32, (8, n), 0)

    def spread(x):
        return jnp.broadcast_to(x, (8, n))

    rows = [d[8 * i:8 * i + 8, :] for i in range(n // 8)]
    done = []
    for b in range(n // 8):
        first = 8 * b
        cols = [spread(rows[b][:, first + k:first + k + 1]) for k in range(8)]
        inside = (lane >= first) & (lane < first + 8)
        w = jnp.where(inside, jnp.where(lane == sub + first, 1.0, 0.0), rows[b])
        lower = w
        scale = jnp.ones((8, n), jnp.float32)
        for k in range(8):
            ip = 1.0 / spread(cols[k][k:k + 1])
            scale = jnp.where(sub == k, ip, scale)
            lower = jnp.where(sub == k, w, lower)
            f = jnp.where(sub == k, 0.0, cols[k] * ip)
            w = w - f * spread(w[k:k + 1])
            for m in range(k + 1, 8):
                cols[m] = cols[m] - f * spread(cols[m][k:k + 1])
        w = w * scale
        done.append(jnp.where(lane <= sub + first, lower, 0.0) * jnp.sqrt(scale))
        ws = [spread(w[m:m + 1]) for m in range(8)]
        for i in range(b + 1, n // 8):
            left = jnp.where(inside, 0.0, rows[i])
            for m in range(8):
                left = left - spread(rows[i][:, first + m:first + m + 1]) * ws[m]
            rows[i] = left
    return jnp.concatenate(done, axis=0)


def dot32(x, y, dims=NN):
    return lax.dot_general(x, y, dims, precision=HIGHEST, preferred_element_type=jnp.float32)


def factor_kernel(
    row_count, col_count, panel_per,
    normal, corner, epiece,
    factor,
    s, panel, edge, panel_send, panel_recv, edge_send, edge_recv,
):
    me = Place(row_count, col_count)
    n = s.shape[0]
    own = n // col_count
    blocks = row_count // col_count
    greet(me)
    for b in range(blocks):
        panel[me.c, b * panel_per:(b + 1) * panel_per, :] = normal[2 * b * panel_per:(2 * b + 1) * panel_per, :]
    source = me.c == me.chip

    @pl.when(source)
    def _():
        edge[me.core] = epiece[...]

    greeted(me)
    peers = [
        me.at(plane, me.ring(k), me.core)
        for k in range(me.y_count) for plane in (me.plane, me.other)
    ][1:]

    def edge_copy(k, g):
        return copy_to(edge.at[me.core], edge.at[me.core], edge_send.at[k], edge_recv.at[me.core], g, me.c)

    @pl.when(source)
    def _():
        for k, peer in enumerate(peers):
            edge_copy(k, peer).start()

    sends = []
    for k in range(1, col_count):
        cp = copy_to(
            panel.at[me.c], panel.at[me.c], panel_send.at[k], panel_recv.at[me.c],
            me.g, lax.rem(me.c + k, col_count),
        )
        cp.start()
        sends.append(cp)

    row_id = lax.broadcasted_iota(jnp.int32, (n, n), 0)
    col_id = lax.broadcasted_iota(jnp.int32, (n, n), 1)
    wide = n // BLOCK
    high = panel_per // 8
    for i in range(high):
        for j in range(wide):
            t = i * wide + j
            for g in range(row_count):
                s[g * panel_per + 8 * i:g * panel_per + 8 * i + 8, j * BLOCK:(j + 1) * BLOCK] = corner[g, t]
    given = s[...]
    s[...] = 0.5 * (given + jnp.transpose(given)) + jnp.where(row_id == col_id, DIAGONAL_SHIFT, 0.0)

    def step(k, _):
        at = pl.ds(pl.multiple_of(k * BLOCK, BLOCK), BLOCK)
        inverse = invert_block(s[at, at])
        below = lax.broadcasted_iota(jnp.int32, (n, BLOCK), 0) >= (k + 1) * BLOCK
        column = jnp.where(below, dot32(s[:, at], inverse, NT), 0.0)
        s[at, at] = jnp.where(
            lax.broadcasted_iota(jnp.int32, (BLOCK, BLOCK), 0) == lax.broadcasted_iota(jnp.int32, (BLOCK, BLOCK), 1),
            1.0, 0.0,
        )
        row = dot32(inverse, s[at, :])
        s[at, :] = row
        s[:, at] = jnp.where(below, 0.0, s[:, at])
        s[...] = s[...] - dot32(column, row)

        @pl.when(k == 0)
        def _():
            @pl.when(jnp.logical_not(source))
            def _():
                edge_copy(0, me.g).wait_recv()

            edge_copy(len(peers), me.sibling).start()

        return 0

    lax.fori_loop(0, wide, step, 0)
    s[...] = jnp.where(col_id <= row_id, s[...], 0.0)
    inverse = s[...]
    across = 1 - me.core
    copy_to(edge.at[across], edge.at[across], edge_send.at[0], edge_recv.at[across], me.g, me.c).wait_recv()
    given_edge = jnp.concatenate(
        [edge[:, i * wide + j].reshape(CORES, 1, 8, BLOCK) for i in range(high) for j in range(wide)], axis=1
    )
    rows_edge = jnp.concatenate(
        [
            jnp.concatenate([given_edge[k, i * wide + j] for j in range(wide)], axis=1)
            for k in range(CORES) for i in range(high)
        ],
        axis=0,
    )
    turned = dot32(rows_edge, inverse, NT)
    weights = jnp.concatenate(
        [s[pl.ds(pl.multiple_of(me.c * own, own), own), :], dot32(turned, inverse)], axis=0
    )
    for k in range(1, col_count):
        t = lax.rem(me.c + k, col_count)
        copy_to(panel.at[t], panel.at[t], panel_send.at[0], panel_recv.at[t], me.g, me.c).wait_recv()
    made = dot32(weights, panel[...].reshape(n, panel.shape[2]))
    for b in range(blocks):
        at = b * panel_per
        factor[2 * at:2 * at + panel_per, :] = made[at:at + panel_per]
        factor[2 * at + panel_per:2 * at + 2 * panel_per, :] = (
            normal[2 * at + panel_per:2 * at + 2 * panel_per, :] - made[own + at:own + at + panel_per]
        )

    @pl.when(source)
    def _():
        for k, peer in enumerate(peers):
            edge_copy(k, peer).wait_send()

    edge_copy(len(peers), me.sibling).wait_send()
    for cp in sends:
        cp.wait_send()


def shards(row_count, col_count, coefficients, tile_mask, duals, costs, primal, fixed):
    rows, columns = coefficients.shape
    panel_per = PANEL // row_count
    window = 2 * panel_per
    blocks = row_count // col_count
    mine = blocks * window
    yc = row_count // (CORES * PLANES)
    half = col_count // 2
    own = PANEL // col_count
    assert blocks == CORES and half == (panel_per // 8) * (PANEL // BLOCK)
    vmem, anywhere = (pl.BlockSpec(memory_space=m) for m in (pltpu.VMEM, pl.ANY))
    dma = pltpu.SemaphoreType.DMA
    f32, bf16 = jnp.float32, jnp.bfloat16
    normal, corner, epiece = pl.pallas_call(
        functools.partial(window_kernel, row_count, col_count, panel_per),
        out_shape=(
            jax.ShapeDtypeStruct((mine, rows), f32),
            jax.ShapeDtypeStruct((row_count, half, 8, BLOCK), f32),
            jax.ShapeDtypeStruct((half, 8, BLOCK), f32),
        ),
        in_specs=[anywhere] * 6,
        out_specs=(vmem,) * 3,
        scratch_shapes=[
            pltpu.VMEM((rows, columns), bf16),
            pltpu.VMEM((row_count, window, columns), bf16),
            pltpu.SMEM(tile_mask.shape, jnp.int32),
            pltpu.VMEM((rows // BLOCK, BLOCK), f32),
            pltpu.VMEM((1, columns), f32), pltpu.VMEM((1, columns), f32), pltpu.VMEM((1, columns), jnp.int32),
            pltpu.VMEM((rows, BLOCK), f32),
            pltpu.VMEM((PLANES * CORES, 1, columns), f32),
            pltpu.VMEM((yc, 1, columns), f32),
            pltpu.VMEM((1, columns), f32),
            pltpu.VMEM((4 * mine, rows), f32),
            pltpu.VMEM((mine, rows), f32),
            pltpu.VMEM((col_count, mine, rows), bf16),
            pltpu.VMEM((col_count, mine, rows), bf16),
            pltpu.VMEM((window, PANEL), f32),
            pltpu.VMEM((col_count, 8, BLOCK), f32),
            pltpu.VMEM((col_count, 8, BLOCK), f32),
            dma((7,)),
            dma((row_count,)), dma((row_count,)),
            dma((PLANES * CORES,)), dma((PLANES * CORES,)),
            dma((yc,)), dma((yc,)),
            dma((col_count,)), dma((col_count,)),
            dma((col_count,)), dma((col_count,)),
            dma((col_count,)), dma((half,)),
            dma((1,)), dma((half,)),
            dma((row_count,)), dma((row_count,)),
        ],
        compiler_params=pltpu.CompilerParams(collective_id=0, has_side_effects=True, vmem_limit_bytes=40 << 20),
        name="window",
    )(
        coefficients, tile_mask, duals.reshape(rows // BLOCK, BLOCK), costs.reshape(1, columns),
        primal.reshape(1, columns), fixed.reshape(1, columns),
    )
    factor = pl.pallas_call(
        functools.partial(factor_kernel, row_count, col_count, panel_per),
        out_shape=jax.ShapeDtypeStruct((mine, rows), f32),
        in_specs=[vmem] * 3,
        out_specs=vmem,
        scratch_shapes=[
            pltpu.VMEM((PANEL, PANEL), f32),
            pltpu.VMEM((col_count, own, rows), f32),
            pltpu.VMEM((CORES, half, 8, BLOCK), f32),
            dma((col_count,)), dma((col_count,)),
            dma((row_count // 2,)), dma((CORES,)),
        ],
        compiler_params=pltpu.CompilerParams(collective_id=1, has_side_effects=True, vmem_limit_bytes=32 << 20),
        name="factor",
    )(normal, corner, epiece)
    return normal, factor


def solution(mesh):
    placed = (P("grow", "gcol"), P("grow", "gcol"), P("grow"), P("gcol"), P("gcol"), P("gcol"))
    return jax.shard_map(
        functools.partial(shards, mesh.shape["grow"], mesh.shape["gcol"]),
        mesh=mesh,
        in_specs=placed,
        out_specs=(P("gcol", "grow"), P("gcol", "grow")),
        check_vma=False,
    )
```

```python
import functools

import jax
import jax.numpy as jnp
from jax import lax
from jax.experimental import pallas as pl
from jax.experimental.pallas import tpu as pltpu
from jax.sharding import PartitionSpec as P

PANEL = 512
SOFTNESS = 0.25
DIAGONAL_SHIFT = 0.5
CORES = 2
PLANES = 2
BLOCK = 128
MESH = pl.DeviceIdType.MESH
HIGHEST = lax.Precision.HIGHEST
NT = (((1,), (1,)), ((), ()))
NN = (((1,), (0,)), ((), ()))


def copy_to(src, dst, send_sem, recv_sem, g, c):
    return pltpu.make_async_remote_copy(
        src_ref=src, dst_ref=dst, send_sem=send_sem, recv_sem=recv_sem, device_id=(g, c), device_id_type=MESH
    )


class Place:
    def __init__(self, row_count, col_count):
        self.y_count = row_count // (CORES * PLANES)
        self.row_count, self.col_count = row_count, col_count
        self.g = lax.axis_index("grow")
        self.c = lax.axis_index("gcol")
        self.core = lax.rem(self.g, CORES)
        self.chip = self.g // CORES
        self.y = lax.rem(self.chip, self.y_count)
        self.plane = self.chip // self.y_count
        self.other = 1 - self.plane
        self.sibling = self.at(self.plane, self.y, 1 - self.core)
        self.partner = self.at(self.other, self.y, self.core)

    def at(self, plane, y, core):
        return (plane * self.y_count + y) * CORES + core

    def ring(self, hop):
        return lax.rem(self.y + hop + 2 * self.y_count, self.y_count)


def greet(me):
    barrier = pltpu.get_barrier_semaphore()
    for k in range(1, me.row_count):
        pl.semaphore_signal(barrier, inc=1, device_id=(lax.rem(me.g + k, me.row_count), me.c), device_id_type=MESH)
    for k in range(1, me.col_count):
        pl.semaphore_signal(barrier, inc=1, device_id=(me.g, lax.rem(me.c + k, me.col_count)), device_id_type=MESH)


def greeted(me):
    pl.semaphore_wait(pltpu.get_barrier_semaphore(), me.row_count + me.col_count - 2)


def invert_block(d):
    n = d.shape[0]
    lane = lax.broadcasted_iota(jnp.int32, (8, n), 1)
    sub = lax.broadcasted_iota(jnp.int32, (8, n), 0)

    def spread(x):
        return jnp.broadcast_to(x, (8, n))

    rows = [d[8 * i:8 * i + 8, :] for i in range(n // 8)]
    done = []
    for b in range(n // 8):
        first = 8 * b
        cols = [spread(rows[b][:, first + k:first + k + 1]) for k in range(8)]
        inside = (lane >= first) & (lane < first + 8)
        w = jnp.where(inside, jnp.where(lane == sub + first, 1.0, 0.0), rows[b])
        lower = w
        scale = jnp.ones((8, n), jnp.float32)
        for k in range(8):
            ip = 1.0 / spread(cols[k][k:k + 1])
            scale = jnp.where(sub == k, ip, scale)
            lower = jnp.where(sub == k, w, lower)
            f = jnp.where(sub == k, 0.0, cols[k] * ip)
            w = w - f * spread(w[k:k + 1])
            for m in range(k + 1, 8):
                cols[m] = cols[m] - f * spread(cols[m][k:k + 1])
        w = w * scale
        done.append(jnp.where(lane <= sub + first, lower, 0.0) * jnp.sqrt(scale))
        ws = [spread(w[m:m + 1]) for m in range(8)]
        for i in range(b + 1, n // 8):
            left = jnp.where(inside, 0.0, rows[i])
            for m in range(8):
                left = left - spread(rows[i][:, first + m:first + m + 1]) * ws[m]
            rows[i] = left
    return jnp.concatenate(done, axis=0)


def dot32(x, y, dims=NN):
    return lax.dot_general(x, y, dims, precision=HIGHEST, preferred_element_type=jnp.float32)


def step_kernel(
    row_count, col_count, panel_per,
    coef, mask_in, duals_in, costs_in, primal_in, fixed_in,
    normal, factor,
    a, win, mask, duals, costs, primal, fixed, dcol, pa, pb, scale, part, own, out, inc, qacc, qout, qin,
    corner, epiece, s, panel, edge,
    load_sem, win_send, win_recv, pa_send, pa_recv, pb_send, pb_recv, rs_send, rs_recv, q_send, q_recv,
    t_send, t_recv, e_send, e_recv, cor_send, cor_recv, panel_send, panel_recv, edge_send, edge_recv,
):
    me = Place(row_count, col_count)
    rows, columns = a.shape
    window = 2 * panel_per
    tile_rows, tile_cols = mask.shape
    side = rows // tile_rows
    yc = me.y_count
    last = yc // 2

    loads = [
        pltpu.make_async_copy(src, dst, load_sem.at[n])
        for n, (src, dst) in enumerate([
            (mask_in, mask),
            (coef.at[pl.ds(0, window)], a.at[pl.ds(0, window)]),
            (duals_in, duals),
            (coef.at[pl.ds(window, rows - window)], a.at[pl.ds(window, rows - window)]),
            (costs_in, costs), (primal_in, primal), (fixed_in, fixed),
        ])
    ]
    for load in loads:
        load.start()
    greet(me)
    loads[0].wait()
    loads[1].wait()

    def mask_window(k, _):
        sl = pl.ds(pl.multiple_of(k * side, side), side)
        m = mask[0, k].astype(jnp.float32)
        for h in (0, 1):
            win[h, me.g, :, sl] = (
                a[h * panel_per:(h + 1) * panel_per, sl].astype(jnp.float32) * m
            ).astype(jnp.bfloat16)
        return 0

    lax.fori_loop(0, tile_cols, mask_window, 0)
    greeted(me)

    sends = []

    def send_window(h, slot, g):
        cp = copy_to(win.at[h, slot], win.at[h, slot], win_send.at[len(sends)], win_recv.at[h, slot], g, me.c)
        cp.start()
        sends.append(cp)

    def got_window(h, slot):
        copy_to(win.at[h, slot], win.at[h, slot], win_send.at[0], win_recv.at[h, slot], me.g, me.c).wait_recv()

    right = me.at(me.plane, me.ring(1), me.core)
    left = me.at(me.plane, me.ring(-1), me.core)
    reach = ((last, (yc - 1) // 2), ((yc - 1) // 2, last))
    planes = (me.plane, me.other)

    def pass_right(h, kind, hop):
        if hop < reach[kind][0]:
            send_window(h, me.at(planes[kind], me.ring(-hop), me.core), right)

    def pass_left(h, kind, hop):
        if hop < reach[kind][1]:
            send_window(h, me.at(planes[kind], me.ring(hop), me.core), left)

    def begin(h):
        send_window(h, me.g, me.partner)
        pass_right(h, 0, 0)
        pass_left(h, 0, 0)
        send_window(h, me.g, me.sibling)

    def cross(h):
        got_window(h, me.partner)
        pass_right(h, 1, 0)
        pass_left(h, 1, 0)
        send_window(h, me.partner, me.sibling)

    def service(h, hop):
        for kind in (0, 1):
            if hop <= reach[kind][0]:
                slot = me.at(planes[kind], me.ring(-hop), me.core)
                got_window(h, slot)
                pass_right(h, kind, hop)
                send_window(h, slot, me.sibling)
            if hop <= reach[kind][1]:
                slot = me.at(planes[kind], me.ring(hop), me.core)
                got_window(h, slot)
                pass_left(h, kind, hop)
                send_window(h, slot, me.sibling)

    def chips_at(hop):
        chips = []
        for kind in (0, 1):
            if hop <= reach[kind][0]:
                chips.append((planes[kind], me.ring(-hop)))
            if hop and hop <= reach[kind][1]:
                chips.append((planes[kind], me.ring(hop)))
        return chips

    begin(0)

    loads[2].wait()
    for i in range(tile_rows):
        dcol[i * side:(i + 1) * side, :] = jnp.transpose(jnp.broadcast_to(duals[i:i + 1, :], (side, side)))
    loads[3].wait()
    q = me.plane * CORES + me.core

    def products(k, _):
        sl = pl.ds(pl.multiple_of(k * side, side), side)
        total = jnp.zeros((8, side), jnp.float32)
        for i in range(tile_rows):
            block = slice(i * side, (i + 1) * side)
            x = a[block, sl].astype(jnp.float32) * mask[i, k].astype(jnp.float32)
            a[block, sl] = x.astype(jnp.bfloat16)
            total += (x * dcol[block, :]).reshape(side // 8, 8, side).sum(axis=0)
        pa[q, :, sl] = total.sum(axis=0, keepdims=True)
        return 0

    lax.fori_loop(0, tile_cols, products, 0)

    quad = [
        (lax.rem(me.plane + dp, PLANES), lax.rem(me.core + dc, CORES))
        for dp in range(PLANES) for dc in range(CORES) if dp or dc
    ]
    for n, (plane, core) in enumerate(quad):
        copy_to(pa.at[q], pa.at[q], pa_send.at[n], pa_recv.at[q], me.at(plane, me.y, core), me.c).start()
    cross(0)
    for plane, core in quad:
        t = plane * CORES + core
        copy_to(pa.at[t], pa.at[t], pa_send.at[0], pa_recv.at[t], me.g, me.c).wait_recv()
    total = pa[0]
    for t in range(1, PLANES * CORES):
        total = total + pa[t]
    pb[me.y] = total
    small = []
    for k in range(1, yc):
        cp = copy_to(
            pb.at[me.y], pb.at[me.y], pb_send.at[k], pb_recv.at[me.y], me.at(me.plane, me.ring(k), me.core), me.c
        )
        cp.start()
        small.append(cp)

    for hop in range(1, last):
        service(0, hop)
    begin(1)
    for k in range(1, yc):
        t = me.ring(k)
        copy_to(pb.at[t], pb.at[t], pb_send.at[0], pb_recv.at[t], me.g, me.c).wait_recv()
    total = pb[0]
    for t in range(1, yc):
        total = total + pb[t]
    for load in loads[4:]:
        load.wait()
    reduced = costs[...] - total
    scale[...] = (1 - fixed[...]).astype(jnp.float32) * primal[...] / jnp.sqrt(reduced * reduced + SOFTNESS)

    def rescale(k, _):
        sl = pl.ds(pl.multiple_of(k * side, side), side)
        x = jnp.broadcast_to(scale[:, sl], (side, side))
        for i in range(tile_rows):
            block = slice(i * side, (i + 1) * side)
            a[block, sl] = (a[block, sl].astype(jnp.float32) * x).astype(jnp.bfloat16)
        return 0

    lax.fori_loop(0, tile_cols, rescale, 0)
    service(0, last)
    cross(1)
    for plane in range(PLANES):
        for y in range(yc):
            got_window(0, me.at(plane, y, 1 - me.core))

    blocks = row_count // col_count
    depth = min(512, columns)
    qacc[...] = jnp.zeros_like(qacc)

    def head(k, _):
        sl = pl.ds(pl.multiple_of(k * depth, depth), depth)
        rhs = win[0, :, :, sl].reshape(row_count * panel_per, depth)
        qacc[...] += lax.dot_general(a[0:window, sl], rhs, NT, preferred_element_type=jnp.float32)
        return 0

    lax.fori_loop(0, columns // depth, head, 0)
    n = s.shape[0]
    wide = n // BLOCK
    high = panel_per // 8
    half = col_count // 2
    for t in range(col_count):
        i, j = t // wide, t % wide
        qout[t] = qacc[8 * i:8 * i + 8, BLOCK * j:BLOCK * j + BLOCK]
    qin[me.c] = qout[me.c]
    for k in range(1, col_count):
        t = lax.rem(me.c + k, col_count)
        copy_to(qout.at[t], qin.at[me.c], q_send.at[k], q_recv.at[me.c], me.g, t).start()

    mine = blocks * panel_per
    for h in (0, 1):
        inc[h, me.c] = jnp.zeros(inc.shape[2:], inc.dtype)

    def multiply(h, owners):
        tall = len(owners) * mine
        part[0:tall, :] = jnp.zeros((tall, rows), jnp.float32)

        def deep(k, _):
            sl = pl.ds(pl.multiple_of(k * depth, depth), depth)
            lhs = jnp.concatenate(
                [win[h, pl.ds(o * blocks, blocks), :, sl].reshape(mine, depth) for o in owners], axis=0
            )
            part[0:tall, :] += lax.dot_general(lhs, a[:, sl], NT, preferred_element_type=jnp.float32)
            return 0

        lax.fori_loop(0, columns // depth, deep, 0)
        for k, owner in enumerate(owners):
            piece = part[k * mine:(k + 1) * mine, :]
            out[h, owner] = piece.astype(jnp.bfloat16)

            @pl.when(owner == me.c)
            def _():
                own[h] = piece

    def scatter(h, owners):
        for owner in owners:
            @pl.when(owner != me.c)
            def _():
                copy_to(
                    out.at[h, owner], inc.at[h, me.c], rs_send.at[h, owner], rs_recv.at[h, me.c], me.g, owner
                ).start()

    def multiply_trailing(hops):
        chips = [chip for hop in hops for chip in chips_at(hop)]
        for plane, y in chips:
            got_window(1, me.at(plane, y, 1 - me.core))
        if chips:
            multiply(1, [plane * yc + y for plane, y in chips])

    def gathered(h):
        for t in range(col_count):
            @pl.when(me.c != t)
            def _():
                copy_to(out.at[h, t], inc.at[h, t], rs_send.at[h, t], rs_recv.at[h, t], me.g, me.c).wait_recv()

        total = own[h]
        for t in range(col_count):
            total = total + inc[h, t].astype(jnp.float32)
        return total

    def trailing_service(hop):
        if hop <= last:
            service(1, hop)

    group = col_count // 2
    start = lax.rem(me.c, 2) * group
    owners = [start + k for k in range(group)]
    multiply(0, owners)
    scatter(0, owners)
    trailing_service(1)

    for k in range(1, col_count):
        t = lax.rem(me.c + k, col_count)
        copy_to(qin.at[t], qin.at[t], q_send.at[0], q_recv.at[t], me.g, me.c).wait_recv()
    tile = qin[0]
    for t in range(1, col_count):
        tile = tile + qin[t]
    in_corner = me.c < half
    home = me.chip

    @pl.when(in_corner)
    def _():
        corner[me.g, me.c] = tile
        for k in range(1, col_count):
            copy_to(
                corner.at[me.g, me.c], corner.at[me.g, me.c], t_send.at[k], t_recv.at[me.c],
                me.g, lax.rem(me.c + k, col_count),
            ).start()

    @pl.when(jnp.logical_not(in_corner))
    def _():
        epiece[me.c - half] = tile

        @pl.when(me.c != home)
        def _():
            copy_to(
                epiece.at[me.c - half], epiece.at[me.c - half], e_send.at[0], e_recv.at[me.c - half], me.g, home
            ).start()

    start = group - start
    owners = [start + k for k in range(group)]
    multiply(0, owners)
    scatter(0, owners)
    trailing_service(2)
    for t in range(half):
        @pl.when(me.c != t)
        def _():
            copy_to(corner.at[me.g, t], corner.at[me.g, t], t_send.at[0], t_recv.at[t], me.g, me.c).wait_recv()

    cor = []

    def send_corner(slot, g):
        cp = copy_to(corner.at[slot], corner.at[slot], cor_send.at[len(cor)], cor_recv.at[slot], g, me.c)
        cp.start()
        cor.append(cp)

    def got_corner(slot):
        copy_to(corner.at[slot], corner.at[slot], cor_send.at[0], cor_recv.at[slot], me.g, me.c).wait_recv()

    for k in range(1, yc):
        send_corner(me.g, me.at(me.plane, me.ring(k), me.core))
    send_corner(me.g, me.partner)
    send_corner(me.g, me.sibling)
    trailing_service(3)
    for k in range(1, yc):
        slot = me.at(me.plane, me.ring(k), me.core)
        got_corner(slot)
        send_corner(slot, me.partner)
        send_corner(slot, me.sibling)
    for hop in range(4, last + 1):
        trailing_service(hop)
    multiply_trailing(range(0, last - 1))
    for k in range(yc):
        slot = me.at(me.other, me.ring(k), me.core)
        got_corner(slot)
        send_corner(slot, me.sibling)
    multiply_trailing(range(last - 1, last + 1))

    source = me.c == home
    peers = [
        me.at(plane, me.ring(k), me.core) for k in range(yc) for plane in (me.plane, me.other)
    ][1:]

    def edge_copy(k, g):
        return copy_to(edge.at[me.core], edge.at[me.core], edge_send.at[k], edge_recv.at[me.core], g, me.c)

    @pl.when(source)
    def _():
        for t in range(half):
            @pl.when(me.c != half + t)
            def _():
                copy_to(epiece.at[t], epiece.at[t], e_send.at[0], e_recv.at[t], me.g, me.c).wait_recv()

        edge[me.core] = epiece[...]
        for k, peer in enumerate(peers):
            edge_copy(k, peer).start()

    panel[me.c] = gathered(0)
    zc = col_count // 2
    x_lo = lax.rem(me.c, 2)
    z = me.c // 2
    across = z * 2 + (1 - x_lo)
    far = []
    for k in range(1, zc // 2 + 1):
        far += [k, zc - k] if k != zc - k else [k]

    def send_panel(k, slot, c):
        copy_to(panel.at[slot], panel.at[slot], panel_send.at[k], panel_recv.at[slot], me.g, c).start()

    def got_panel(slot):
        copy_to(panel.at[slot], panel.at[slot], panel_send.at[0], panel_recv.at[slot], me.g, me.c).wait_recv()

    send_panel(0, me.c, across)
    for k in far:
        send_panel(k, me.c, lax.rem(z + k, zc) * 2 + x_lo)

    scatter(1, [lax.rem(me.c + k, col_count) for k in range(1, col_count)])

    def pass_panel(first, stop):
        for k in far[first:stop]:
            slot = lax.rem(z - k + zc, zc) * 2 + x_lo
            got_panel(slot)
            send_panel(zc + k, slot, across)

    for plane in range(PLANES):
        for y in range(yc):
            got_corner(me.at(plane, y, 1 - me.core))

    row_id = lax.broadcasted_iota(jnp.int32, (n, n), 0)
    col_id = lax.broadcasted_iota(jnp.int32, (n, n), 1)
    for i in range(high):
        for j in range(wide):
            t = i * wide + j
            for g in range(row_count):
                s[g * panel_per + 8 * i:g * panel_per + 8 * i + 8, j * BLOCK:(j + 1) * BLOCK] = corner[g, t]
    given = s[...]
    s[...] = 0.5 * (given + jnp.transpose(given)) + jnp.where(row_id == col_id, DIAGONAL_SHIFT, 0.0)

    def step(k, _):
        at = pl.ds(pl.multiple_of(k * BLOCK, BLOCK), BLOCK)
        inverse = invert_block(s[at, at])
        s[at, at] = inverse
        for m in range(wide):
            @pl.when(k == m)
            def _():
                lo, hi = m * BLOCK, (m + 1) * BLOCK
                inverse = s[lo:hi, lo:hi]
                if m:
                    s[lo:hi, 0:lo] = dot32(inverse, s[lo:hi, 0:lo])
                if hi < n:
                    column = dot32(s[hi:n, lo:hi], inverse, NT)
                    s[hi:n, lo:hi] = jnp.zeros((n - hi, BLOCK), jnp.float32)
                    s[lo:hi, hi:n] = dot32(inverse, s[lo:hi, hi:n])
                    s[hi:n, :] = s[hi:n, :] - dot32(column, s[lo:hi, :])

        cuts = [len(far) * m // 3 for m in range(4)]
        for m in range(min(3, wide)):
            @pl.when(k == m)
            def _():
                pass_panel(cuts[m], cuts[m + 1] if m + 1 < wide else len(far))
                if m == 0:
                    @pl.when(jnp.logical_not(source))
                    def _():
                        edge_copy(0, me.g).wait_recv()

                    edge_copy(len(peers), me.sibling).start()

        return 0

    lax.fori_loop(0, wide, step, 0)
    s[...] = jnp.where(col_id <= row_id, s[...], 0.0)
    inverse = s[...]
    over = 1 - me.core
    copy_to(edge.at[over], edge.at[over], edge_send.at[0], edge_recv.at[over], me.g, me.c).wait_recv()
    rows_edge = jnp.concatenate(
        [
            jnp.concatenate([edge[k, i * wide + j] for j in range(wide)], axis=1)
            for k in range(CORES) for i in range(high)
        ],
        axis=0,
    )
    turned = dot32(rows_edge, inverse, NT)
    weights = jnp.concatenate(
        [s[pl.ds(pl.multiple_of(me.c * mine, mine), mine), :], dot32(turned, inverse)], axis=0
    )
    for k in range(zc):
        got_panel(k * 2 + 1 - x_lo)
    made = dot32(weights, panel[...].reshape(n, rows))
    trailing = gathered(1)
    for b in range(blocks):
        at = b * panel_per
        p = slice(2 * at, 2 * at + panel_per)
        t = slice(2 * at + panel_per, 2 * at + 2 * panel_per)
        normal[p, :] = panel[me.c, at:at + panel_per, :]
        normal[t, :] = trailing[at:at + panel_per]
        factor[p, :] = made[at:at + panel_per]
        factor[t, :] = trailing[at:at + panel_per] - made[mine + at:mine + at + panel_per]

    @pl.when(source)
    def _():
        for k, peer in enumerate(peers):
            edge_copy(k, peer).wait_send()

    edge_copy(len(peers), me.sibling).wait_send()

    @pl.when(jnp.logical_not(in_corner) & (me.c != home))
    def _():
        copy_to(epiece.at[0], epiece.at[0], e_send.at[0], e_recv.at[0], me.g, home).wait_send()

    @pl.when(in_corner)
    def _():
        for k in range(1, col_count):
            copy_to(qout.at[0], qout.at[0], t_send.at[k], t_recv.at[0], me.g, me.c).wait_send()

    for h in (0, 1):
        for t in range(col_count):
            @pl.when(me.c != t)
            def _():
                copy_to(out.at[h, t], inc.at[h, t], rs_send.at[h, t], rs_recv.at[h, t], me.g, me.c).wait_send()
    for k in range(1, col_count):
        copy_to(qout.at[0], qout.at[0], q_send.at[k], q_recv.at[0], me.g, me.c).wait_send()
    for k in range(len(quad)):
        copy_to(pa.at[0], pa.at[0], pa_send.at[k], pa_recv.at[0], me.g, me.c).wait_send()
    for k in [0] + far + [zc + k for k in far]:
        copy_to(panel.at[0], panel.at[0], panel_send.at[k], panel_recv.at[0], me.g, me.c).wait_send()
    for cp in small + sends + cor:
        cp.wait_send()


def shards(row_count, col_count, coefficients, tile_mask, duals, costs, primal, fixed):
    rows, columns = coefficients.shape
    panel_per = PANEL // row_count
    window = 2 * panel_per
    blocks = row_count // col_count
    mine = blocks * panel_per
    yc = row_count // (CORES * PLANES)
    half = col_count // 2
    assert blocks == CORES and half == (panel_per // 8) * (PANEL // BLOCK)
    vmem, hbm = (pl.BlockSpec(memory_space=m) for m in (pltpu.VMEM, pltpu.HBM))
    dma = pltpu.SemaphoreType.DMA
    f32, bf16 = jnp.float32, jnp.bfloat16
    return pl.pallas_call(
        functools.partial(step_kernel, row_count, col_count, panel_per),
        out_shape=(jax.ShapeDtypeStruct((2 * mine, rows), f32),) * 2,
        in_specs=[hbm] * 6,
        out_specs=(vmem,) * 2,
        scratch_shapes=[
            pltpu.VMEM((rows, columns), bf16),
            pltpu.VMEM((2, row_count, panel_per, columns), bf16),
            pltpu.SMEM(tile_mask.shape, jnp.int32),
            pltpu.VMEM((rows // BLOCK, BLOCK), f32),
            pltpu.VMEM((1, columns), f32), pltpu.VMEM((1, columns), f32), pltpu.VMEM((1, columns), jnp.int32),
            pltpu.VMEM((rows, BLOCK), f32),
            pltpu.VMEM((PLANES * CORES, 1, columns), f32),
            pltpu.VMEM((yc, 1, columns), f32),
            pltpu.VMEM((1, columns), f32),
            pltpu.VMEM((col_count * mine, rows), f32),
            pltpu.VMEM((2, mine, rows), f32),
            pltpu.VMEM((2, col_count, mine, rows), bf16),
            pltpu.VMEM((2, col_count, mine, rows), bf16),
            pltpu.VMEM((window, PANEL), f32),
            pltpu.VMEM((col_count, 8, BLOCK), f32),
            pltpu.VMEM((col_count, 8, BLOCK), f32),
            pltpu.VMEM((row_count, half, 8, BLOCK), f32),
            pltpu.VMEM((half, 8, BLOCK), f32),
            pltpu.VMEM((PANEL, PANEL), f32),
            pltpu.VMEM((col_count, mine, rows), f32),
            pltpu.VMEM((CORES, half, 8, BLOCK), f32),
            dma((7,)),
            dma((2 * row_count,)), dma((2, row_count)),
            dma((PLANES * CORES,)), dma((PLANES * CORES,)),
            dma((yc,)), dma((yc,)),
            dma((2, col_count)), dma((2, col_count)),
            dma((col_count,)), dma((col_count,)),
            dma((col_count,)), dma((half,)),
            dma((1,)), dma((half,)),
            dma((row_count,)), dma((row_count,)),
            dma((col_count,)), dma((col_count,)),
            dma((row_count // 2,)), dma((CORES,)),
        ],
        compiler_params=pltpu.CompilerParams(collective_id=0, has_side_effects=True, vmem_limit_bytes=60 << 20),
        name="window_step",
    )(
        coefficients, tile_mask, duals.reshape(rows // BLOCK, BLOCK), costs.reshape(1, columns),
        primal.reshape(1, columns), fixed.reshape(1, columns),
    )


def solution(mesh):
    placed = (P("grow", "gcol"), P("grow", "gcol"), P("grow"), P("gcol"), P("gcol"), P("gcol"))
    return jax.shard_map(
        functools.partial(shards, mesh.shape["grow"], mesh.shape["gcol"]),
        mesh=mesh,
        in_specs=placed,
        out_specs=(P("gcol", "grow"), P("gcol", "grow")),
        check_vma=False,
    )
```

```python
import functools

import jax
import jax.numpy as jnp
from jax import lax
from jax.experimental import pallas as pl
from jax.experimental.pallas import tpu as pltpu
from jax.sharding import PartitionSpec as P

PANEL = 512
SOFTNESS = 0.25
DIAGONAL_SHIFT = 0.5
CORES = 2
PLANES = 2
BLOCK = 128
MESH = pl.DeviceIdType.MESH
HIGHEST = lax.Precision.HIGHEST
NT = (((1,), (1,)), ((), ()))
NN = (((1,), (0,)), ((), ()))


def copy_to(src, dst, send_sem, recv_sem, g, c):
    return pltpu.make_async_remote_copy(
        src_ref=src, dst_ref=dst, send_sem=send_sem, recv_sem=recv_sem, device_id=(g, c), device_id_type=MESH
    )


class Place:
    def __init__(self, row_count, col_count):
        self.y_count = row_count // (CORES * PLANES)
        self.row_count, self.col_count = row_count, col_count
        self.g = lax.axis_index("grow")
        self.c = lax.axis_index("gcol")
        self.core = lax.rem(self.g, CORES)
        self.chip = self.g // CORES
        self.y = lax.rem(self.chip, self.y_count)
        self.plane = self.chip // self.y_count
        self.other = 1 - self.plane
        self.sibling = self.at(self.plane, self.y, 1 - self.core)
        self.partner = self.at(self.other, self.y, self.core)

    def at(self, plane, y, core):
        return (plane * self.y_count + y) * CORES + core

    def ring(self, hop):
        return lax.rem(self.y + hop + 2 * self.y_count, self.y_count)


def greet(me):
    barrier = pltpu.get_barrier_semaphore()
    for k in range(1, me.row_count):
        pl.semaphore_signal(barrier, inc=1, device_id=(lax.rem(me.g + k, me.row_count), me.c), device_id_type=MESH)
    for k in range(1, me.col_count):
        pl.semaphore_signal(barrier, inc=1, device_id=(me.g, lax.rem(me.c + k, me.col_count)), device_id_type=MESH)


def greeted(me):
    pl.semaphore_wait(pltpu.get_barrier_semaphore(), me.row_count + me.col_count - 2)


def invert_block(d):
    n = d.shape[0]
    lane = lax.broadcasted_iota(jnp.int32, (8, n), 1)
    sub = lax.broadcasted_iota(jnp.int32, (8, n), 0)

    def spread(x):
        return jnp.broadcast_to(x, (8, n))

    rows = [d[8 * i:8 * i + 8, :] for i in range(n // 8)]
    done = []
    for b in range(n // 8):
        first = 8 * b
        cols = [spread(rows[b][:, first + k:first + k + 1]) for k in range(8)]
        inside = (lane >= first) & (lane < first + 8)
        w = jnp.where(inside, jnp.where(lane == sub + first, 1.0, 0.0), rows[b])
        lower = w
        scale = jnp.ones((8, n), jnp.float32)
        for k in range(8):
            ip = 1.0 / spread(cols[k][k:k + 1])
            scale = jnp.where(sub == k, ip, scale)
            lower = jnp.where(sub == k, w, lower)
            f = jnp.where(sub == k, 0.0, cols[k] * ip)
            w = w - f * spread(w[k:k + 1])
            for m in range(k + 1, 8):
                cols[m] = cols[m] - f * spread(cols[m][k:k + 1])
        w = w * scale
        done.append(jnp.where(lane <= sub + first, lower, 0.0) * jnp.sqrt(scale))
        ws = [spread(w[m:m + 1]) for m in range(8)]
        for i in range(b + 1, n // 8):
            left = jnp.where(inside, 0.0, rows[i])
            for m in range(8):
                left = left - spread(rows[i][:, first + m:first + m + 1]) * ws[m]
            rows[i] = left
    return jnp.concatenate(done, axis=0)


def dot32(x, y, dims=NN):
    return lax.dot_general(x, y, dims, precision=HIGHEST, preferred_element_type=jnp.float32)


def step_kernel(
    row_count, col_count, panel_per,
    coef, mask_in, duals_in, costs_in, primal_in, fixed_in,
    normal, factor,
    a, win, mask, duals, costs, primal, fixed, dcol, pa, pb, scale, part, pair, out_x, in_x, out_z, in_z,
    qacc, qout, qin,
    corner, epiece, s, panel, edge,
    load_sem, win_send, win_recv, pa_send, pa_recv, pb_send, pb_recv, x_send, x_recv, z_send, z_recv, q_send, q_recv,
    t_send, t_recv, e_send, e_recv, cor_send, cor_recv, panel_send, panel_recv, edge_send, edge_recv,
):
    me = Place(row_count, col_count)
    rows, columns = a.shape
    window = 2 * panel_per
    tile_rows, tile_cols = mask.shape
    side = rows // tile_rows
    yc = me.y_count
    last = yc // 2

    loads = [
        pltpu.make_async_copy(src, dst, load_sem.at[n])
        for n, (src, dst) in enumerate([
            (mask_in, mask),
            (coef.at[pl.ds(0, window)], a.at[pl.ds(0, window)]),
            (duals_in, duals),
            (coef.at[pl.ds(window, rows - window)], a.at[pl.ds(window, rows - window)]),
            (costs_in, costs), (primal_in, primal), (fixed_in, fixed),
        ])
    ]
    for load in loads:
        load.start()
    greet(me)
    loads[0].wait()
    loads[1].wait()

    def mask_window(k, _):
        sl = pl.ds(pl.multiple_of(k * side, side), side)
        m = mask[0, k].astype(jnp.float32)
        for h in (0, 1):
            win[h, me.g, :, sl] = (
                a[h * panel_per:(h + 1) * panel_per, sl].astype(jnp.float32) * m
            ).astype(jnp.bfloat16)
        return 0

    lax.fori_loop(0, tile_cols, mask_window, 0)
    greeted(me)

    sends = []

    def send_window(h, slot, g):
        cp = copy_to(win.at[h, slot], win.at[h, slot], win_send.at[len(sends)], win_recv.at[h, slot], g, me.c)
        cp.start()
        sends.append(cp)

    def got_window(h, slot):
        copy_to(win.at[h, slot], win.at[h, slot], win_send.at[0], win_recv.at[h, slot], me.g, me.c).wait_recv()

    right = me.at(me.plane, me.ring(1), me.core)
    left = me.at(me.plane, me.ring(-1), me.core)
    reach = ((last, (yc - 1) // 2), ((yc - 1) // 2, last))
    planes = (me.plane, me.other)

    def pass_right(h, kind, hop):
        if hop < reach[kind][0]:
            send_window(h, me.at(planes[kind], me.ring(-hop), me.core), right)

    def pass_left(h, kind, hop):
        if hop < reach[kind][1]:
            send_window(h, me.at(planes[kind], me.ring(hop), me.core), left)

    def begin(h):
        send_window(h, me.g, me.partner)
        pass_right(h, 0, 0)
        pass_left(h, 0, 0)
        send_window(h, me.g, me.sibling)

    def cross(h):
        got_window(h, me.partner)
        pass_right(h, 1, 0)
        pass_left(h, 1, 0)
        send_window(h, me.partner, me.sibling)

    def service(h, hop):
        for kind in (0, 1):
            if hop <= reach[kind][0]:
                slot = me.at(planes[kind], me.ring(-hop), me.core)
                got_window(h, slot)
                pass_right(h, kind, hop)
                send_window(h, slot, me.sibling)
            if hop <= reach[kind][1]:
                slot = me.at(planes[kind], me.ring(hop), me.core)
                got_window(h, slot)
                pass_left(h, kind, hop)
                send_window(h, slot, me.sibling)

    begin(0)

    loads[2].wait()
    for i in range(tile_rows):
        dcol[i * side:(i + 1) * side, :] = jnp.transpose(jnp.broadcast_to(duals[i:i + 1, :], (side, side)))
    loads[3].wait()
    q = me.plane * CORES + me.core

    def products(k, _):
        sl = pl.ds(pl.multiple_of(k * side, side), side)
        total = jnp.zeros((8, side), jnp.float32)
        for i in range(tile_rows):
            block = slice(i * side, (i + 1) * side)
            x = a[block, sl].astype(jnp.float32) * mask[i, k].astype(jnp.float32)
            a[block, sl] = x.astype(jnp.bfloat16)
            total += (x * dcol[block, :]).reshape(side // 8, 8, side).sum(axis=0)
        pa[q, :, sl] = total.sum(axis=0, keepdims=True)
        return 0

    lax.fori_loop(0, tile_cols, products, 0)

    quad = [
        (lax.rem(me.plane + dp, PLANES), lax.rem(me.core + dc, CORES))
        for dp in range(PLANES) for dc in range(CORES) if dp or dc
    ]
    for n, (plane, core) in enumerate(quad):
        copy_to(pa.at[q], pa.at[q], pa_send.at[n], pa_recv.at[q], me.at(plane, me.y, core), me.c).start()
    cross(0)
    for plane, core in quad:
        t = plane * CORES + core
        copy_to(pa.at[t], pa.at[t], pa_send.at[0], pa_recv.at[t], me.g, me.c).wait_recv()
    total = pa[0]
    for t in range(1, PLANES * CORES):
        total = total + pa[t]
    pb[me.y] = total
    small = []
    for k in range(1, yc):
        cp = copy_to(
            pb.at[me.y], pb.at[me.y], pb_send.at[k], pb_recv.at[me.y], me.at(me.plane, me.ring(k), me.core), me.c
        )
        cp.start()
        small.append(cp)

    for hop in range(1, last):
        service(0, hop)
    begin(1)
    for k in range(1, yc):
        t = me.ring(k)
        copy_to(pb.at[t], pb.at[t], pb_send.at[0], pb_recv.at[t], me.g, me.c).wait_recv()
    total = pb[0]
    for t in range(1, yc):
        total = total + pb[t]
    for load in loads[4:]:
        load.wait()
    reduced = costs[...] - total
    scale[...] = (1 - fixed[...]).astype(jnp.float32) * primal[...] / jnp.sqrt(reduced * reduced + SOFTNESS)

    def rescale(k, _):
        sl = pl.ds(pl.multiple_of(k * side, side), side)
        x = jnp.broadcast_to(scale[:, sl], (side, side))
        for i in range(tile_rows):
            block = slice(i * side, (i + 1) * side)
            a[block, sl] = (a[block, sl].astype(jnp.float32) * x).astype(jnp.bfloat16)
        return 0

    lax.fori_loop(0, tile_cols, rescale, 0)
    service(0, last)
    cross(1)
    for plane in range(PLANES):
        for y in range(yc):
            got_window(0, me.at(plane, y, 1 - me.core))

    blocks = row_count // col_count
    depth = min(512, columns)
    qacc[...] = jnp.zeros_like(qacc)

    def head(k, _):
        sl = pl.ds(pl.multiple_of(k * depth, depth), depth)
        rhs = win[0, :, :, sl].reshape(row_count * panel_per, depth)
        qacc[...] += lax.dot_general(a[0:window, sl], rhs, NT, preferred_element_type=jnp.float32)
        return 0

    lax.fori_loop(0, columns // depth, head, 0)
    n = s.shape[0]
    wide = n // BLOCK
    high = panel_per // 8
    half = col_count // 2
    for t in range(col_count):
        i, j = t // wide, t % wide
        qout[t] = qacc[8 * i:8 * i + 8, BLOCK * j:BLOCK * j + BLOCK]
    qin[me.c] = qout[me.c]
    for k in range(1, col_count):
        t = lax.rem(me.c + k, col_count)
        copy_to(qout.at[t], qin.at[me.c], q_send.at[k], q_recv.at[me.c], me.g, t).start()

    mine = blocks * panel_per
    zc = col_count // 2
    x_lo = lax.rem(me.c, 2)
    z = me.c // 2
    across = z * 2 + (1 - x_lo)

    def multiply(h, x):
        part[...] = jnp.zeros_like(part)

        def deep(k, _):
            sl = pl.ds(pl.multiple_of(k * depth, depth), depth)
            lhs = jnp.concatenate(
                [win[h, pl.ds((t * 2 + x) * blocks, blocks), :, sl].reshape(mine, depth) for t in range(zc)], axis=0
            )
            part[...] += lax.dot_general(lhs, a[:, sl], NT, preferred_element_type=jnp.float32)
            return 0

        lax.fori_loop(0, columns // depth, deep, 0)

    def pair_copy(h):
        return copy_to(out_x.at[h], in_x.at[h], x_send.at[h], x_recv.at[h], me.g, across)

    def scatter_pair(h):
        multiply(h, 1 - x_lo)
        for t in range(zc):
            out_x[h, t] = part[t * mine:(t + 1) * mine, :].astype(jnp.bfloat16)
        pair_copy(h).start()

    def keep(h):
        multiply(h, x_lo)
        for t in range(zc):
            pair[h, t] = part[t * mine:(t + 1) * mine, :]

    def scatter(h):
        pair_copy(h).wait_recv()
        for t in range(zc):
            both = pair[h, t] + in_x[h, t].astype(jnp.float32)
            pair[h, t] = both
            out_z[h, t] = both.astype(jnp.bfloat16)
        for k in range(1, zc):
            t = lax.rem(z + k, zc)
            copy_to(out_z.at[h, t], in_z.at[h, z], z_send.at[h, t], z_recv.at[h, z], me.g, t * 2 + x_lo).start()

    def gathered(h):
        total = pair[h, z]
        for k in range(1, zc):
            t = lax.rem(z + k, zc)
            copy_to(out_z.at[h, t], in_z.at[h, t], z_send.at[h, t], z_recv.at[h, t], me.g, me.c).wait_recv()
            total = total + in_z[h, t].astype(jnp.float32)
        return total

    def trailing_service(hop):
        if hop <= last:
            service(1, hop)

    scatter_pair(0)

    for k in range(1, col_count):
        t = lax.rem(me.c + k, col_count)
        copy_to(qin.at[t], qin.at[t], q_send.at[0], q_recv.at[t], me.g, me.c).wait_recv()
    tile = qin[0]
    for t in range(1, col_count):
        tile = tile + qin[t]
    in_corner = me.c < half
    home = me.chip

    @pl.when(in_corner)
    def _():
        corner[me.g, me.c] = tile
        for k in range(1, col_count):
            copy_to(
                corner.at[me.g, me.c], corner.at[me.g, me.c], t_send.at[k], t_recv.at[me.c],
                me.g, lax.rem(me.c + k, col_count),
            ).start()

    @pl.when(jnp.logical_not(in_corner))
    def _():
        epiece[me.c - half] = tile

        @pl.when(me.c != home)
        def _():
            copy_to(
                epiece.at[me.c - half], epiece.at[me.c - half], e_send.at[0], e_recv.at[me.c - half], me.g, home
            ).start()

    trailing_service(1)
    keep(0)
    scatter(0)
    trailing_service(2)
    for t in range(half):
        @pl.when(me.c != t)
        def _():
            copy_to(corner.at[me.g, t], corner.at[me.g, t], t_send.at[0], t_recv.at[t], me.g, me.c).wait_recv()

    cor = []

    def send_corner(slot, g):
        cp = copy_to(corner.at[slot], corner.at[slot], cor_send.at[len(cor)], cor_recv.at[slot], g, me.c)
        cp.start()
        cor.append(cp)

    def got_corner(slot):
        copy_to(corner.at[slot], corner.at[slot], cor_send.at[0], cor_recv.at[slot], me.g, me.c).wait_recv()

    for k in range(1, yc):
        send_corner(me.g, me.at(me.plane, me.ring(k), me.core))
    send_corner(me.g, me.partner)
    send_corner(me.g, me.sibling)
    trailing_service(3)
    for k in range(1, yc):
        slot = me.at(me.plane, me.ring(k), me.core)
        got_corner(slot)
        send_corner(slot, me.partner)
        send_corner(slot, me.sibling)
    for k in range(yc):
        slot = me.at(me.other, me.ring(k), me.core)
        got_corner(slot)
        send_corner(slot, me.sibling)

    source = me.c == home
    peers = [
        me.at(plane, me.ring(k), me.core) for k in range(yc) for plane in (me.plane, me.other)
    ][1:]

    def edge_copy(k, g):
        return copy_to(edge.at[me.core], edge.at[me.core], edge_send.at[k], edge_recv.at[me.core], g, me.c)

    @pl.when(source)
    def _():
        for t in range(half):
            @pl.when(me.c != half + t)
            def _():
                copy_to(epiece.at[t], epiece.at[t], e_send.at[0], e_recv.at[t], me.g, me.c).wait_recv()

        edge[me.core] = epiece[...]
        for k, peer in enumerate(peers):
            edge_copy(k, peer).start()

    panel[me.c] = gathered(0)
    far = []
    for k in range(1, zc // 2 + 1):
        far += [k, zc - k] if k != zc - k else [k]

    def send_panel(k, slot, c):
        copy_to(panel.at[slot], panel.at[slot], panel_send.at[k], panel_recv.at[slot], me.g, c).start()

    def got_panel(slot):
        copy_to(panel.at[slot], panel.at[slot], panel_send.at[0], panel_recv.at[slot], me.g, me.c).wait_recv()

    send_panel(0, me.c, across)
    for k in far:
        send_panel(k, me.c, lax.rem(z + k, zc) * 2 + x_lo)


    def pass_panel(first, stop):
        for k in far[first:stop]:
            slot = lax.rem(z - k + zc, zc) * 2 + x_lo
            got_panel(slot)
            send_panel(zc + k, slot, across)

    for plane in range(PLANES):
        for y in range(yc):
            got_corner(me.at(plane, y, 1 - me.core))
    for hop in range(4, last + 1):
        trailing_service(hop)

    row_id = lax.broadcasted_iota(jnp.int32, (n, n), 0)
    col_id = lax.broadcasted_iota(jnp.int32, (n, n), 1)
    for i in range(high):
        for j in range(wide):
            t = i * wide + j
            for g in range(row_count):
                s[g * panel_per + 8 * i:g * panel_per + 8 * i + 8, j * BLOCK:(j + 1) * BLOCK] = corner[g, t]
    given = s[...]
    s[...] = 0.5 * (given + jnp.transpose(given)) + jnp.where(row_id == col_id, DIAGONAL_SHIFT, 0.0)

    def step(k, _):
        at = pl.ds(pl.multiple_of(k * BLOCK, BLOCK), BLOCK)
        inverse = invert_block(s[at, at])
        s[at, at] = inverse
        for m in range(wide):
            @pl.when(k == m)
            def _():
                lo, hi = m * BLOCK, (m + 1) * BLOCK
                inverse = s[lo:hi, lo:hi]
                if m:
                    s[lo:hi, 0:lo] = dot32(inverse, s[lo:hi, 0:lo])
                if hi < n:
                    column = dot32(s[hi:n, lo:hi], inverse, NT)
                    s[hi:n, lo:hi] = jnp.zeros((n - hi, BLOCK), jnp.float32)
                    s[lo:hi, hi:n] = dot32(inverse, s[lo:hi, hi:n])
                    s[hi:n, :] = s[hi:n, :] - dot32(column, s[lo:hi, :])

        cuts = [len(far) * m // 3 for m in range(4)]
        for m in range(min(3, wide)):
            @pl.when(k == m)
            def _():
                pass_panel(cuts[m], cuts[m + 1] if m + 1 < wide else len(far))
                if m == 0:
                    @pl.when(jnp.logical_not(source))
                    def _():
                        edge_copy(0, me.g).wait_recv()

                    edge_copy(len(peers), me.sibling).start()

        @pl.when(k == 0)
        def _():
            for plane in range(PLANES):
                for y in range(yc):
                    got_window(1, me.at(plane, y, 1 - me.core))
            scatter_pair(1)

        @pl.when(k == min(1, wide - 1))
        def _():
            keep(1)
            scatter(1)

        return 0

    lax.fori_loop(0, wide, step, 0)
    s[...] = jnp.where(col_id <= row_id, s[...], 0.0)
    inverse = s[...]
    over = 1 - me.core
    copy_to(edge.at[over], edge.at[over], edge_send.at[0], edge_recv.at[over], me.g, me.c).wait_recv()
    rows_edge = jnp.concatenate(
        [
            jnp.concatenate([edge[k, i * wide + j] for j in range(wide)], axis=1)
            for k in range(CORES) for i in range(high)
        ],
        axis=0,
    )
    turned = dot32(rows_edge, inverse, NT)
    weights = jnp.concatenate(
        [s[pl.ds(pl.multiple_of(me.c * mine, mine), mine), :], dot32(turned, inverse)], axis=0
    )
    for k in range(zc):
        got_panel(k * 2 + 1 - x_lo)
    made = dot32(weights, panel[...].reshape(n, rows))
    trailing = gathered(1)
    for b in range(blocks):
        at = b * panel_per
        p = slice(2 * at, 2 * at + panel_per)
        t = slice(2 * at + panel_per, 2 * at + 2 * panel_per)
        normal[p, :] = panel[me.c, at:at + panel_per, :]
        normal[t, :] = trailing[at:at + panel_per]
        factor[p, :] = made[at:at + panel_per]
        factor[t, :] = trailing[at:at + panel_per] - made[mine + at:mine + at + panel_per]

    @pl.when(source)
    def _():
        for k, peer in enumerate(peers):
            edge_copy(k, peer).wait_send()

    edge_copy(len(peers), me.sibling).wait_send()

    @pl.when(jnp.logical_not(in_corner) & (me.c != home))
    def _():
        copy_to(epiece.at[0], epiece.at[0], e_send.at[0], e_recv.at[0], me.g, home).wait_send()

    @pl.when(in_corner)
    def _():
        for k in range(1, col_count):
            copy_to(qout.at[0], qout.at[0], t_send.at[k], t_recv.at[0], me.g, me.c).wait_send()

    for h in (0, 1):
        pair_copy(h).wait_send()
        for k in range(1, zc):
            t = lax.rem(z + k, zc)
            copy_to(out_z.at[h, t], in_z.at[h, t], z_send.at[h, t], z_recv.at[h, t], me.g, me.c).wait_send()
    for k in range(1, col_count):
        copy_to(qout.at[0], qout.at[0], q_send.at[k], q_recv.at[0], me.g, me.c).wait_send()
    for k in range(len(quad)):
        copy_to(pa.at[0], pa.at[0], pa_send.at[k], pa_recv.at[0], me.g, me.c).wait_send()
    for k in [0] + far + [zc + k for k in far]:
        copy_to(panel.at[0], panel.at[0], panel_send.at[k], panel_recv.at[0], me.g, me.c).wait_send()
    for cp in small + sends + cor:
        cp.wait_send()


def shards(row_count, col_count, coefficients, tile_mask, duals, costs, primal, fixed):
    rows, columns = coefficients.shape
    panel_per = PANEL // row_count
    window = 2 * panel_per
    blocks = row_count // col_count
    mine = blocks * panel_per
    yc = row_count // (CORES * PLANES)
    half = col_count // 2
    assert blocks == CORES and half == (panel_per // 8) * (PANEL // BLOCK)
    vmem, hbm = (pl.BlockSpec(memory_space=m) for m in (pltpu.VMEM, pltpu.HBM))
    dma = pltpu.SemaphoreType.DMA
    f32, bf16 = jnp.float32, jnp.bfloat16
    return pl.pallas_call(
        functools.partial(step_kernel, row_count, col_count, panel_per),
        out_shape=(jax.ShapeDtypeStruct((2 * mine, rows), f32),) * 2,
        in_specs=[hbm] * 6,
        out_specs=(vmem,) * 2,
        scratch_shapes=[
            pltpu.VMEM((rows, columns), bf16),
            pltpu.VMEM((2, row_count, panel_per, columns), bf16),
            pltpu.SMEM(tile_mask.shape, jnp.int32),
            pltpu.VMEM((rows // BLOCK, BLOCK), f32),
            pltpu.VMEM((1, columns), f32), pltpu.VMEM((1, columns), f32), pltpu.VMEM((1, columns), jnp.int32),
            pltpu.VMEM((rows, BLOCK), f32),
            pltpu.VMEM((PLANES * CORES, 1, columns), f32),
            pltpu.VMEM((yc, 1, columns), f32),
            pltpu.VMEM((1, columns), f32),
            pltpu.VMEM((half * mine, rows), f32),
            pltpu.VMEM((2, half, mine, rows), f32),
            pltpu.VMEM((2, half, mine, rows), bf16),
            pltpu.VMEM((2, half, mine, rows), bf16),
            pltpu.VMEM((2, half, mine, rows), bf16),
            pltpu.VMEM((2, half, mine, rows), bf16),
            pltpu.VMEM((window, PANEL), f32),
            pltpu.VMEM((col_count, 8, BLOCK), f32),
            pltpu.VMEM((col_count, 8, BLOCK), f32),
            pltpu.VMEM((row_count, half, 8, BLOCK), f32),
            pltpu.VMEM((half, 8, BLOCK), f32),
            pltpu.VMEM((PANEL, PANEL), f32),
            pltpu.VMEM((col_count, mine, rows), f32),
            pltpu.VMEM((CORES, half, 8, BLOCK), f32),
            dma((7,)),
            dma((2 * row_count,)), dma((2, row_count)),
            dma((PLANES * CORES,)), dma((PLANES * CORES,)),
            dma((yc,)), dma((yc,)),
            dma((2,)), dma((2,)),
            dma((2, half)), dma((2, half)),
            dma((col_count,)), dma((col_count,)),
            dma((col_count,)), dma((half,)),
            dma((1,)), dma((half,)),
            dma((row_count,)), dma((row_count,)),
            dma((col_count,)), dma((col_count,)),
            dma((row_count // 2,)), dma((CORES,)),
        ],
        compiler_params=pltpu.CompilerParams(collective_id=0, has_side_effects=True, vmem_limit_bytes=60 << 20),
        name="window_step",
    )(
        coefficients, tile_mask, duals.reshape(rows // BLOCK, BLOCK), costs.reshape(1, columns),
        primal.reshape(1, columns), fixed.reshape(1, columns),
    )


def solution(mesh):
    placed = (P("grow", "gcol"), P("grow", "gcol"), P("grow"), P("gcol"), P("gcol"), P("gcol"))
    return jax.shard_map(
        functools.partial(shards, mesh.shape["grow"], mesh.shape["gcol"]),
        mesh=mesh,
        in_specs=placed,
        out_specs=(P("gcol", "grow"), P("gcol", "grow")),
        check_vma=False,
    )
```

```python
import functools

import jax
import jax.numpy as jnp
from jax import lax
from jax.experimental import pallas as pl
from jax.experimental.pallas import tpu as pltpu
from jax.sharding import PartitionSpec as P

PANEL = 512
SOFTNESS = 0.25
DIAGONAL_SHIFT = 0.5
CORES = 2
PLANES = 2
BLOCK = 128
MESH = pl.DeviceIdType.MESH
HIGHEST = lax.Precision.HIGHEST
NT = (((1,), (1,)), ((), ()))
NN = (((1,), (0,)), ((), ()))


def copy_to(src, dst, send_sem, recv_sem, g, c):
    return pltpu.make_async_remote_copy(
        src_ref=src, dst_ref=dst, send_sem=send_sem, recv_sem=recv_sem, device_id=(g, c), device_id_type=MESH
    )


class Place:
    def __init__(self, row_count, col_count):
        self.y_count = row_count // (CORES * PLANES)
        self.row_count, self.col_count = row_count, col_count
        self.g = lax.axis_index("grow")
        self.c = lax.axis_index("gcol")
        self.core = lax.rem(self.g, CORES)
        self.chip = self.g // CORES
        self.y = lax.rem(self.chip, self.y_count)
        self.plane = self.chip // self.y_count
        self.other = 1 - self.plane
        self.sibling = self.at(self.plane, self.y, 1 - self.core)
        self.partner = self.at(self.other, self.y, self.core)

    def at(self, plane, y, core):
        return (plane * self.y_count + y) * CORES + core

    def ring(self, hop):
        return lax.rem(self.y + hop + 2 * self.y_count, self.y_count)


def greet(me):
    barrier = pltpu.get_barrier_semaphore()
    for k in range(1, me.row_count):
        pl.semaphore_signal(barrier, inc=1, device_id=(lax.rem(me.g + k, me.row_count), me.c), device_id_type=MESH)
    for k in range(1, me.col_count):
        pl.semaphore_signal(barrier, inc=1, device_id=(me.g, lax.rem(me.c + k, me.col_count)), device_id_type=MESH)


def greeted(me):
    pl.semaphore_wait(pltpu.get_barrier_semaphore(), me.row_count + me.col_count - 2)


def invert_block(d):
    n = d.shape[0]
    lane = lax.broadcasted_iota(jnp.int32, (8, n), 1)
    sub = lax.broadcasted_iota(jnp.int32, (8, n), 0)

    def spread(x):
        return jnp.broadcast_to(x, (8, n))

    rows = [d[8 * i:8 * i + 8, :] for i in range(n // 8)]
    done = []
    for b in range(n // 8):
        first = 8 * b
        cols = [spread(rows[b][:, first + k:first + k + 1]) for k in range(8)]
        inside = (lane >= first) & (lane < first + 8)
        w = jnp.where(inside, jnp.where(lane == sub + first, 1.0, 0.0), rows[b])
        lower = w
        scale = jnp.ones((8, n), jnp.float32)
        for k in range(8):
            ip = 1.0 / spread(cols[k][k:k + 1])
            scale = jnp.where(sub == k, ip, scale)
            lower = jnp.where(sub == k, w, lower)
            f = jnp.where(sub == k, 0.0, cols[k] * ip)
            w = w - f * spread(w[k:k + 1])
            for m in range(k + 1, 8):
                cols[m] = cols[m] - f * spread(cols[m][k:k + 1])
        w = w * scale
        done.append(jnp.where(lane <= sub + first, lower, 0.0) * jnp.sqrt(scale))
        ws = [spread(w[m:m + 1]) for m in range(8)]
        for i in range(b + 1, n // 8):
            left = jnp.where(inside, 0.0, rows[i])
            for m in range(8):
                left = left - spread(rows[i][:, first + m:first + m + 1]) * ws[m]
            rows[i] = left
    return jnp.concatenate(done, axis=0)


def dot32(x, y, dims=NN):
    return lax.dot_general(x, y, dims, precision=HIGHEST, preferred_element_type=jnp.float32)


def step_kernel(
    row_count, col_count, panel_per,
    coef, mask_in, duals_in, costs_in, primal_in, fixed_in,
    normal, factor,
    a, win, mask, duals, costs, primal, fixed, dcol, pa, pb, scale, part, pair, out_x, in_x, out_z, in_z,
    qacc, qout, qin,
    corner, epiece, s, panel, edge,
    load_sem, win_send, win_recv, pa_send, pa_recv, pb_send, pb_recv, x_send, x_recv, z_send, z_recv, q_send, q_recv,
    t_send, t_recv, e_send, e_recv, cor_send, cor_recv, panel_send, panel_recv, edge_send, edge_recv,
):
    me = Place(row_count, col_count)
    rows, columns = a.shape
    window = 2 * panel_per
    tile_rows, tile_cols = mask.shape
    side = rows // tile_rows
    yc = me.y_count
    last = yc // 2

    loads = [
        pltpu.make_async_copy(src, dst, load_sem.at[n])
        for n, (src, dst) in enumerate([
            (mask_in, mask),
            (coef.at[pl.ds(0, window)], a.at[pl.ds(0, window)]),
            (duals_in, duals),
            (coef.at[pl.ds(window, rows - window)], a.at[pl.ds(window, rows - window)]),
            (costs_in, costs), (primal_in, primal), (fixed_in, fixed),
        ])
    ]
    for load in loads:
        load.start()
    greet(me)
    loads[0].wait()
    loads[1].wait()

    def mask_window(k, _):
        sl = pl.ds(pl.multiple_of(k * side, side), side)
        m = mask[0, k].astype(jnp.float32)
        for h in (0, 1):
            win[h, me.g, :, sl] = (
                a[h * panel_per:(h + 1) * panel_per, sl].astype(jnp.float32) * m
            ).astype(jnp.bfloat16)
        return 0

    lax.fori_loop(0, tile_cols, mask_window, 0)
    greeted(me)

    sends = []

    def send_window(h, slot, g):
        cp = copy_to(win.at[h, slot], win.at[h, slot], win_send.at[len(sends)], win_recv.at[h, slot], g, me.c)
        cp.start()
        sends.append(cp)

    def got_window(h, slot):
        copy_to(win.at[h, slot], win.at[h, slot], win_send.at[0], win_recv.at[h, slot], me.g, me.c).wait_recv()

    right = me.at(me.plane, me.ring(1), me.core)
    left = me.at(me.plane, me.ring(-1), me.core)
    reach = ((last, (yc - 1) // 2), ((yc - 1) // 2, last))
    planes = (me.plane, me.other)

    def pass_right(h, kind, hop):
        if hop < reach[kind][0]:
            send_window(h, me.at(planes[kind], me.ring(-hop), me.core), right)

    def pass_left(h, kind, hop):
        if hop < reach[kind][1]:
            send_window(h, me.at(planes[kind], me.ring(hop), me.core), left)

    def begin(h):
        send_window(h, me.g, me.partner)
        pass_right(h, 0, 0)
        pass_left(h, 0, 0)
        send_window(h, me.g, me.sibling)

    def cross(h):
        got_window(h, me.partner)
        pass_right(h, 1, 0)
        pass_left(h, 1, 0)
        send_window(h, me.partner, me.sibling)

    def service(h, hop):
        for kind in (0, 1):
            if hop <= reach[kind][0]:
                slot = me.at(planes[kind], me.ring(-hop), me.core)
                got_window(h, slot)
                pass_right(h, kind, hop)
                send_window(h, slot, me.sibling)
            if hop <= reach[kind][1]:
                slot = me.at(planes[kind], me.ring(hop), me.core)
                got_window(h, slot)
                pass_left(h, kind, hop)
                send_window(h, slot, me.sibling)

    begin(0)

    loads[2].wait()
    for i in range(tile_rows):
        dcol[i * side:(i + 1) * side, :] = jnp.transpose(jnp.broadcast_to(duals[i:i + 1, :], (side, side)))
    loads[3].wait()
    q = me.plane * CORES + me.core

    def products(k, _):
        sl = pl.ds(pl.multiple_of(k * side, side), side)
        total = jnp.zeros((8, side), jnp.float32)
        for i in range(tile_rows):
            block = slice(i * side, (i + 1) * side)
            x = a[block, sl].astype(jnp.float32) * mask[i, k].astype(jnp.float32)
            a[block, sl] = x.astype(jnp.bfloat16)
            total += (x * dcol[block, :]).reshape(side // 8, 8, side).sum(axis=0)
        pa[q, :, sl] = total.sum(axis=0, keepdims=True)
        return 0

    lax.fori_loop(0, tile_cols, products, 0)

    quad = [
        (lax.rem(me.plane + dp, PLANES), lax.rem(me.core + dc, CORES))
        for dp in range(PLANES) for dc in range(CORES) if dp or dc
    ]
    for n, (plane, core) in enumerate(quad):
        copy_to(pa.at[q], pa.at[q], pa_send.at[n], pa_recv.at[q], me.at(plane, me.y, core), me.c).start()
    cross(0)
    for plane, core in quad:
        t = plane * CORES + core
        copy_to(pa.at[t], pa.at[t], pa_send.at[0], pa_recv.at[t], me.g, me.c).wait_recv()
    total = pa[0]
    for t in range(1, PLANES * CORES):
        total = total + pa[t]
    pb[me.y] = total
    small = []
    for k in range(1, yc):
        cp = copy_to(
            pb.at[me.y], pb.at[me.y], pb_send.at[k], pb_recv.at[me.y], me.at(me.plane, me.ring(k), me.core), me.c
        )
        cp.start()
        small.append(cp)

    for hop in range(1, last):
        service(0, hop)
    begin(1)
    for k in range(1, yc):
        t = me.ring(k)
        copy_to(pb.at[t], pb.at[t], pb_send.at[0], pb_recv.at[t], me.g, me.c).wait_recv()
    total = pb[0]
    for t in range(1, yc):
        total = total + pb[t]
    for load in loads[4:]:
        load.wait()
    reduced = costs[...] - total
    scale[...] = (1 - fixed[...]).astype(jnp.float32) * primal[...] / jnp.sqrt(reduced * reduced + SOFTNESS)

    def rescale(k, _):
        sl = pl.ds(pl.multiple_of(k * side, side), side)
        x = jnp.broadcast_to(scale[:, sl], (side, side))
        for i in range(tile_rows):
            block = slice(i * side, (i + 1) * side)
            a[block, sl] = (a[block, sl].astype(jnp.float32) * x).astype(jnp.bfloat16)
        return 0

    lax.fori_loop(0, tile_cols, rescale, 0)
    service(0, last)
    cross(1)
    for plane in range(PLANES):
        for y in range(yc):
            got_window(0, me.at(plane, y, 1 - me.core))

    blocks = row_count // col_count
    depth = min(512, columns)
    qacc[...] = jnp.zeros_like(qacc)

    def head(k, _):
        sl = pl.ds(pl.multiple_of(k * depth, depth), depth)
        rhs = win[0, :, :, sl].reshape(row_count * panel_per, depth)
        qacc[...] += lax.dot_general(a[0:window, sl], rhs, NT, preferred_element_type=jnp.float32)
        return 0

    lax.fori_loop(0, columns // depth, head, 0)
    n = s.shape[0]
    wide = n // BLOCK
    high = panel_per // 8
    half = col_count // 2
    for t in range(col_count):
        i, j = t // wide, t % wide
        qout[t] = qacc[8 * i:8 * i + 8, BLOCK * j:BLOCK * j + BLOCK]
    qin[me.c] = qout[me.c]
    for k in range(1, col_count):
        t = lax.rem(me.c + k, col_count)
        copy_to(qout.at[t], qin.at[me.c], q_send.at[k], q_recv.at[me.c], me.g, t).start()

    mine = blocks * panel_per
    zc = col_count // 2
    x_lo = lax.rem(me.c, 2)
    z = me.c // 2
    across = z * 2 + (1 - x_lo)

    def multiply(h, x):
        part[...] = jnp.zeros_like(part)

        def deep(k, _):
            sl = pl.ds(pl.multiple_of(k * depth, depth), depth)
            lhs = jnp.concatenate(
                [win[h, pl.ds((t * 2 + x) * blocks, blocks), :, sl].reshape(mine, depth) for t in range(zc)], axis=0
            )
            part[...] += lax.dot_general(lhs, a[:, sl], NT, preferred_element_type=jnp.float32)
            return 0

        lax.fori_loop(0, columns // depth, deep, 0)

    def pair_copy(h):
        return copy_to(out_x.at[h], in_x.at[h], x_send.at[h], x_recv.at[h], me.g, across)

    def make_pair(h):
        multiply(h, 1 - x_lo)
        for t in range(zc):
            out_x[h, t] = part[t * mine:(t + 1) * mine, :].astype(jnp.bfloat16)

    def keep(h):
        multiply(h, x_lo)
        for t in range(zc):
            pair[h, t] = part[t * mine:(t + 1) * mine, :]

    def scatter(h):
        pair_copy(h).wait_recv()
        for t in range(zc):
            both = pair[h, t] + in_x[h, t].astype(jnp.float32)
            pair[h, t] = both
            out_z[h, t] = both.astype(jnp.bfloat16)
        for k in range(1, zc):
            t = lax.rem(z + k, zc)
            copy_to(out_z.at[h, t], in_z.at[h, z], z_send.at[h, t], z_recv.at[h, z], me.g, t * 2 + x_lo).start()

    def gathered(h):
        total = pair[h, z]
        for k in range(1, zc):
            t = lax.rem(z + k, zc)
            copy_to(out_z.at[h, t], in_z.at[h, t], z_send.at[h, t], z_recv.at[h, t], me.g, me.c).wait_recv()
            total = total + in_z[h, t].astype(jnp.float32)
        return total

    def trailing_service(hop):
        if hop <= last:
            service(1, hop)

    make_pair(0)

    for k in range(1, col_count):
        t = lax.rem(me.c + k, col_count)
        copy_to(qin.at[t], qin.at[t], q_send.at[0], q_recv.at[t], me.g, me.c).wait_recv()
    tile = qin[0]
    for t in range(1, col_count):
        tile = tile + qin[t]
    in_corner = me.c < half
    home = me.chip

    @pl.when(in_corner)
    def _():
        corner[me.g, me.c] = tile
        for k in range(1, col_count):
            copy_to(
                corner.at[me.g, me.c], corner.at[me.g, me.c], t_send.at[k], t_recv.at[me.c],
                me.g, lax.rem(me.c + k, col_count),
            ).start()

    @pl.when(jnp.logical_not(in_corner))
    def _():
        epiece[me.c - half] = tile

        @pl.when(me.c != home)
        def _():
            copy_to(
                epiece.at[me.c - half], epiece.at[me.c - half], e_send.at[0], e_recv.at[me.c - half], me.g, home
            ).start()

    pair_copy(0).start()
    trailing_service(1)
    keep(0)
    for t in range(half):
        @pl.when(me.c != t)
        def _():
            copy_to(corner.at[me.g, t], corner.at[me.g, t], t_send.at[0], t_recv.at[t], me.g, me.c).wait_recv()

    cor = []

    def send_corner(slot, g):
        cp = copy_to(corner.at[slot], corner.at[slot], cor_send.at[len(cor)], cor_recv.at[slot], g, me.c)
        cp.start()
        cor.append(cp)

    def got_corner(slot):
        copy_to(corner.at[slot], corner.at[slot], cor_send.at[0], cor_recv.at[slot], me.g, me.c).wait_recv()

    for k in range(1, yc):
        send_corner(me.g, me.at(me.plane, me.ring(k), me.core))
    send_corner(me.g, me.partner)
    send_corner(me.g, me.sibling)
    trailing_service(2)
    scatter(0)
    trailing_service(3)
    for k in range(1, yc):
        slot = me.at(me.plane, me.ring(k), me.core)
        got_corner(slot)
        send_corner(slot, me.partner)
        send_corner(slot, me.sibling)
    for k in range(yc):
        slot = me.at(me.other, me.ring(k), me.core)
        got_corner(slot)
        send_corner(slot, me.sibling)

    source = me.c == home
    peers = [
        me.at(plane, me.ring(k), me.core) for k in range(yc) for plane in (me.plane, me.other)
    ][1:]

    def edge_copy(k, g):
        return copy_to(edge.at[me.core], edge.at[me.core], edge_send.at[k], edge_recv.at[me.core], g, me.c)

    @pl.when(source)
    def _():
        for t in range(half):
            @pl.when(me.c != half + t)
            def _():
                copy_to(epiece.at[t], epiece.at[t], e_send.at[0], e_recv.at[t], me.g, me.c).wait_recv()

        edge[me.core] = epiece[...]
        for k, peer in enumerate(peers):
            edge_copy(k, peer).start()

    panel[me.c] = gathered(0)
    far = []
    for k in range(1, zc // 2 + 1):
        far += [k, zc - k] if k != zc - k else [k]

    def send_panel(k, slot, c):
        copy_to(panel.at[slot], panel.at[slot], panel_send.at[k], panel_recv.at[slot], me.g, c).start()

    def got_panel(slot):
        copy_to(panel.at[slot], panel.at[slot], panel_send.at[0], panel_recv.at[slot], me.g, me.c).wait_recv()

    send_panel(0, me.c, across)
    for k in far:
        send_panel(k, me.c, lax.rem(z + k, zc) * 2 + x_lo)


    def pass_panel(first, stop):
        for k in far[first:stop]:
            slot = lax.rem(z - k + zc, zc) * 2 + x_lo
            got_panel(slot)
            send_panel(zc + k, slot, across)

    for plane in range(PLANES):
        for y in range(yc):
            got_corner(me.at(plane, y, 1 - me.core))
    for hop in range(4, last + 1):
        trailing_service(hop)

    row_id = lax.broadcasted_iota(jnp.int32, (n, n), 0)
    col_id = lax.broadcasted_iota(jnp.int32, (n, n), 1)
    for i in range(high):
        for j in range(wide):
            t = i * wide + j
            for g in range(row_count):
                s[g * panel_per + 8 * i:g * panel_per + 8 * i + 8, j * BLOCK:(j + 1) * BLOCK] = corner[g, t]
    given = s[...]
    s[...] = 0.5 * (given + jnp.transpose(given)) + jnp.where(row_id == col_id, DIAGONAL_SHIFT, 0.0)

    def step(k, _):
        at = pl.ds(pl.multiple_of(k * BLOCK, BLOCK), BLOCK)
        inverse = invert_block(s[at, at])
        s[at, at] = inverse
        for m in range(wide):
            @pl.when(k == m)
            def _():
                lo, hi = m * BLOCK, (m + 1) * BLOCK
                inverse = s[lo:hi, lo:hi]
                if m:
                    s[lo:hi, 0:lo] = dot32(inverse, s[lo:hi, 0:lo])
                if hi < n:
                    column = dot32(s[hi:n, lo:hi], inverse, NT)
                    s[hi:n, lo:hi] = jnp.zeros((n - hi, BLOCK), jnp.float32)
                    s[lo:hi, hi:n] = dot32(inverse, s[lo:hi, hi:n])
                    s[hi:n, :] = s[hi:n, :] - dot32(column, s[lo:hi, :])

        cuts = [len(far) * m // 3 for m in range(4)]
        for m in range(min(3, wide)):
            @pl.when(k == m)
            def _():
                pass_panel(cuts[m], cuts[m + 1] if m + 1 < wide else len(far))
                if m == 0:
                    @pl.when(jnp.logical_not(source))
                    def _():
                        edge_copy(0, me.g).wait_recv()

                    edge_copy(len(peers), me.sibling).start()

        @pl.when(k == 0)
        def _():
            for plane in range(PLANES):
                for y in range(yc):
                    got_window(1, me.at(plane, y, 1 - me.core))
            make_pair(1)
            pair_copy(1).start()

        @pl.when(k == min(1, wide - 1))
        def _():
            keep(1)
            scatter(1)

        return 0

    lax.fori_loop(0, wide, step, 0)
    s[...] = jnp.where(col_id <= row_id, s[...], 0.0)
    inverse = s[...]
    over = 1 - me.core
    copy_to(edge.at[over], edge.at[over], edge_send.at[0], edge_recv.at[over], me.g, me.c).wait_recv()
    rows_edge = jnp.concatenate(
        [
            jnp.concatenate([edge[k, i * wide + j] for j in range(wide)], axis=1)
            for k in range(CORES) for i in range(high)
        ],
        axis=0,
    )
    turned = dot32(rows_edge, inverse, NT)
    weights = jnp.concatenate(
        [s[pl.ds(pl.multiple_of(me.c * mine, mine), mine), :], dot32(turned, inverse)], axis=0
    )
    for k in range(zc):
        got_panel(k * 2 + 1 - x_lo)
    made = dot32(weights, panel[...].reshape(n, rows))
    trailing = gathered(1)
    for b in range(blocks):
        at = b * panel_per
        p = slice(2 * at, 2 * at + panel_per)
        t = slice(2 * at + panel_per, 2 * at + 2 * panel_per)
        normal[p, :] = panel[me.c, at:at + panel_per, :]
        normal[t, :] = trailing[at:at + panel_per]
        factor[p, :] = made[at:at + panel_per]
        factor[t, :] = trailing[at:at + panel_per] - made[mine + at:mine + at + panel_per]

    @pl.when(source)
    def _():
        for k, peer in enumerate(peers):
            edge_copy(k, peer).wait_send()

    edge_copy(len(peers), me.sibling).wait_send()

    @pl.when(jnp.logical_not(in_corner) & (me.c != home))
    def _():
        copy_to(epiece.at[0], epiece.at[0], e_send.at[0], e_recv.at[0], me.g, home).wait_send()

    @pl.when(in_corner)
    def _():
        for k in range(1, col_count):
            copy_to(qout.at[0], qout.at[0], t_send.at[k], t_recv.at[0], me.g, me.c).wait_send()

    for h in (0, 1):
        pair_copy(h).wait_send()
        for k in range(1, zc):
            t = lax.rem(z + k, zc)
            copy_to(out_z.at[h, t], in_z.at[h, t], z_send.at[h, t], z_recv.at[h, t], me.g, me.c).wait_send()
    for k in range(1, col_count):
        copy_to(qout.at[0], qout.at[0], q_send.at[k], q_recv.at[0], me.g, me.c).wait_send()
    for k in range(len(quad)):
        copy_to(pa.at[0], pa.at[0], pa_send.at[k], pa_recv.at[0], me.g, me.c).wait_send()
    for k in [0] + far + [zc + k for k in far]:
        copy_to(panel.at[0], panel.at[0], panel_send.at[k], panel_recv.at[0], me.g, me.c).wait_send()
    for cp in small + sends + cor:
        cp.wait_send()


def shards(row_count, col_count, coefficients, tile_mask, duals, costs, primal, fixed):
    rows, columns = coefficients.shape
    panel_per = PANEL // row_count
    window = 2 * panel_per
    blocks = row_count // col_count
    mine = blocks * panel_per
    yc = row_count // (CORES * PLANES)
    half = col_count // 2
    assert blocks == CORES and half == (panel_per // 8) * (PANEL // BLOCK)
    vmem, hbm = (pl.BlockSpec(memory_space=m) for m in (pltpu.VMEM, pltpu.HBM))
    dma = pltpu.SemaphoreType.DMA
    f32, bf16 = jnp.float32, jnp.bfloat16
    return pl.pallas_call(
        functools.partial(step_kernel, row_count, col_count, panel_per),
        out_shape=(jax.ShapeDtypeStruct((2 * mine, rows), f32),) * 2,
        in_specs=[hbm] * 6,
        out_specs=(vmem,) * 2,
        scratch_shapes=[
            pltpu.VMEM((rows, columns), bf16),
            pltpu.VMEM((2, row_count, panel_per, columns), bf16),
            pltpu.SMEM(tile_mask.shape, jnp.int32),
            pltpu.VMEM((rows // BLOCK, BLOCK), f32),
            pltpu.VMEM((1, columns), f32), pltpu.VMEM((1, columns), f32), pltpu.VMEM((1, columns), jnp.int32),
            pltpu.VMEM((rows, BLOCK), f32),
            pltpu.VMEM((PLANES * CORES, 1, columns), f32),
            pltpu.VMEM((yc, 1, columns), f32),
            pltpu.VMEM((1, columns), f32),
            pltpu.VMEM((half * mine, rows), f32),
            pltpu.VMEM((2, half, mine, rows), f32),
            pltpu.VMEM((2, half, mine, rows), bf16),
            pltpu.VMEM((2, half, mine, rows), bf16),
            pltpu.VMEM((2, half, mine, rows), bf16),
            pltpu.VMEM((2, half, mine, rows), bf16),
            pltpu.VMEM((window, PANEL), f32),
            pltpu.VMEM((col_count, 8, BLOCK), f32),
            pltpu.VMEM((col_count, 8, BLOCK), f32),
            pltpu.VMEM((row_count, half, 8, BLOCK), f32),
            pltpu.VMEM((half, 8, BLOCK), f32),
            pltpu.VMEM((PANEL, PANEL), f32),
            pltpu.VMEM((col_count, mine, rows), f32),
            pltpu.VMEM((CORES, half, 8, BLOCK), f32),
            dma((7,)),
            dma((2 * row_count,)), dma((2, row_count)),
            dma((PLANES * CORES,)), dma((PLANES * CORES,)),
            dma((yc,)), dma((yc,)),
            dma((2,)), dma((2,)),
            dma((2, half)), dma((2, half)),
            dma((col_count,)), dma((col_count,)),
            dma((col_count,)), dma((half,)),
            dma((1,)), dma((half,)),
            dma((row_count,)), dma((row_count,)),
            dma((col_count,)), dma((col_count,)),
            dma((row_count // 2,)), dma((CORES,)),
        ],
        compiler_params=pltpu.CompilerParams(collective_id=0, has_side_effects=True, vmem_limit_bytes=60 << 20),
        name="window_step",
    )(
        coefficients, tile_mask, duals.reshape(rows // BLOCK, BLOCK), costs.reshape(1, columns),
        primal.reshape(1, columns), fixed.reshape(1, columns),
    )


def solution(mesh):
    placed = (P("grow", "gcol"), P("grow", "gcol"), P("grow"), P("gcol"), P("gcol"), P("gcol"))
    return jax.shard_map(
        functools.partial(shards, mesh.shape["grow"], mesh.shape["gcol"]),
        mesh=mesh,
        in_specs=placed,
        out_specs=(P("gcol", "grow"), P("gcol", "grow")),
        check_vma=False,
    )
```
